256 devices in a mesh: seg: 4 (over x), pitch: 4 (over y), span: 16 (over z, core).
Axes of the slice: x: 4, y: 4, z: 8, core: 2. Of those that a mesh axis runs over, the one named last changes fastest.
Arguments:
- states: float32 [4, 5, 1024, 4096], P('seg', None, 'pitch', 'span'), may hold values from -6 to 6
- forcing: float32 [4, 5, 1024, 4096], P('seg', None, 'pitch', 'span'), may hold values from -6 to 6
- adv_pitch: float32 [5, 5], replicated, may hold values from -2.5 to 2.5
- adv_span: float32 [5, 5], replicated, may hold values from -2.5 to 2.5
- diffusion: float32 [5], replicated, may hold values from 0.1 to 0.4
Outputs:
- mismatch: float32 [4, 5, 1024, 4096], P('seg', None, 'pitch', 'span')
- gradient: float32 [4, 5, 1024, 4096], P('seg', None, 'pitch', 'span')
The draws below stay inside these ranges and needn't reach their ends.
All inputs are finite; a program needn't handle non-finite values.
Results may differ from the reference program's by a relative error of at most 0.0001.
Values sent between devices are 32-bit elements; how exact they have to be, the bound alone decides.
A program may use at most 64 MiB of HBM per device.

```python
import math
import jax
import jax.numpy as jnp
from jax import lax

FIELDS = 5
SUBSTEPS = 2
SEGMENTS = 4
NP = 1024
NS = 4096


def steps_of(key, extent, shards, low, top_value):
    level, own = 1.0, jax.random.fold_in(key, 6)
    for dim, parts in shards:
        heights = jnp.exp(jax.random.uniform(jax.random.fold_in(own, dim), (parts,), jnp.float32, low / len(shards), top_value / len(shards)))
        level = level * jnp.repeat(heights, extent[dim] // parts).reshape([-1 if axis == dim else 1 for axis in range(len(extent))])
    return level


def bell_draw(rng, shape, scale, bound, cuts=(), dtype=jnp.bfloat16):
    array = scale * jax.random.normal(rng, shape, jnp.float32)
    if cuts:
        array = array * steps_of(rng, shape, cuts, -0.22, 0.18)
    return jnp.clip(array, -bound, bound).astype(dtype)


def setup_inputs(seed: int = 0) -> dict:
    key_list = jax.random.split(jax.random.key(seed), 6)
    states = bell_draw(key_list[0], (SEGMENTS, FIELDS, NP, NS), 1.0, 6.0, ((0, 4), (2, 4), (3, 16)), jnp.float32)
    forcing = bell_draw(key_list[1], (SEGMENTS, FIELDS, NP, NS), 1.0, 6.0, ((0, 4), (2, 4), (3, 16)), jnp.float32)
    adv_pitch = bell_draw(key_list[2], (FIELDS, FIELDS), FIELDS ** -0.5, 2.5, (), jnp.float32)
    adv_span = bell_draw(key_list[3], (FIELDS, FIELDS), FIELDS ** -0.5, 2.5, (), jnp.float32)
    diffusion = jnp.clip(jnp.exp(jax.random.uniform(key_list[4], (FIELDS,), jnp.float32, math.log(0.1), math.log(0.4))), 0.1, 0.4)
    return {"states": states, "forcing": forcing, "adv_pitch": adv_pitch, "adv_span": adv_span, "diffusion": diffusion}


time_step = 0.25

def substep(field, mat_pitch, mat_span, viscous):
    padded = jnp.pad(field, ((0, 0), (1, 1), (0, 0)), mode='wrap')
    padded = jnp.pad(padded, ((0, 0), (0, 0), (1, 1)))
    centre = padded[:, 1:-1, 1:-1]
    along_pitch = (padded[:, 2:, 1:-1] - padded[:, :-2, 1:-1]) * 0.5
    along_span = (padded[:, 1:-1, 2:] - padded[:, 1:-1, :-2]) * 0.5
    laplace = padded[:, 2:, 1:-1] + padded[:, :-2, 1:-1] + padded[:, 1:-1, 2:] + padded[:, 1:-1, :-2] - 4.0 * centre
    flux = jnp.einsum('fg,gpq->fpq', mat_pitch, along_pitch, precision=lax.Precision.HIGHEST)
    flux = flux + jnp.einsum('fg,gpq->fpq', mat_span, along_span, precision=lax.Precision.HIGHEST)
    return centre + time_step * (flux + viscous[:, None, None] * laplace)

def reference(states, forcing, adv_pitch, adv_span, diffusion):

    def advance(field):
        for repeat in range(SUBSTEPS):
            field = substep(field, -adv_pitch, -adv_span, diffusion)
        return field
    ending = lax.map(advance, states) + time_step * forcing
    mismatch = ending - jnp.roll(states, -1, axis=0)

    def adjoint(residue):
        return jax.vjp(advance, jnp.zeros_like(residue))[1](residue)[0]
    gradient = lax.map(adjoint, mismatch) - jnp.roll(mismatch, 1, axis=0)
    return (mismatch, gradient)
```

```python
import functools

import jax
import jax.numpy as jnp
from jax import lax
from jax.experimental import pallas as pl
from jax.experimental.pallas import tpu as pltpu
from jax.sharding import PartitionSpec as P

MESH = pl.DeviceIdType.MESH
F = 5
L = 128
PAD = 16
CH = 32
M, E, H = 0, 1, 2


def along(axis, by):
    count = lax.axis_size(axis)
    return {axis: lax.rem(lax.axis_index(axis) + (by + count), count)}


def rolled(x, by):
    return pltpu.roll(x, by % L, 1)


def kernel(
    states, forcing, pitch_ref, span_ref, diff_ref, mis_out, grad_out,
    raw, force, v0, v1, w0, w1, end, got_a, got_b, packed, packed2, halo, halo2,
    load_s, load_f, a_send, a_recv, b_send, b_recv, col_send, col_recv, row_send, row_recv,
):
    rows = raw.shape[1]
    chunks = rows // CH
    blocks = rows // 8
    order = [0, chunks - 1] + list(range(1, chunks - 1))

    def load(src, dst, sem, c):
        part = pl.ds(c * CH, CH)
        return pltpu.make_async_copy(src.at[0, :, part], dst.at[:, part], sem.at[c])

    for c in range(chunks):
        load(states, raw, load_s, c).start()
    for c in range(chunks):
        load(forcing, force, load_f, c).start()

    barrier = pltpu.get_barrier_semaphore()
    for axis in ("seg", "pitch", "span"):
        for by in (1, -1):
            pl.semaphore_signal(barrier, inc=1, device_id=along(axis, by), device_id_type=MESH)

    lane = lax.broadcasted_iota(jnp.int32, (8, L), 1)
    low = lane < 64
    span_at, span_of = lax.axis_index("span"), lax.axis_size("span")
    has_left = jnp.where(span_at > 0, 1, 0)
    has_right = jnp.where(span_at < span_of - 1, 1, 0)
    inside = jnp.where(low, has_left, has_right) > 0
    packed_left = (lane & 3) >= 2
    packed_inside = jnp.where(packed_left, has_left, has_right) > 0

    fwd = (
        [[pitch_ref[f, g] * -0.125 for g in range(F)] for f in range(F)],
        [[span_ref[f, g] * -0.125 for g in range(F)] for f in range(F)],
    )
    adj = (
        [[pitch_ref[g, f] * 0.125 for g in range(F)] for f in range(F)],
        [[span_ref[g, f] * 0.125 for g in range(F)] for f in range(F)],
    )
    keep = [1.0 - diff_ref[f] for f in range(F)]
    visc = [diff_ref[f] * 0.25 for f in range(F)]

    def rotate_in(first, second):
        one, two = rolled(first, 64), rolled(second, 64)
        return jnp.where(low, one, two), jnp.where(low, two, one)

    def rotate_out(mid, edge):
        one, two = rolled(mid, 64), rolled(edge, 64)
        return jnp.where(low, two, one), jnp.where(low, one, two)

    def stencil(src, mats, e, outs, seam):
        along_pitch, along_span = mats
        total = {t: [None] * F for t in outs}
        for g in range(F):
            here, left, right = {}, {}, {}
            for t in (M, E, H):
                if (t == H and not seam) or (t == M and E not in outs and M not in outs):
                    continue
                here[t] = src[t, g, pl.ds(e, 8), :]
                right[t] = rolled(here[t], -1)
                left[t] = rolled(here[t], 1)
            for t in outs:
                if t == M:
                    rt = jnp.where(lane == 127, right[E], right[M])
                    lf = jnp.where(lane == 0, left[E], left[M])
                elif t == E:
                    rt = jnp.where(lane == 127, right[M], right[E])
                    lf = jnp.where(lane == 0, left[M], left[E])
                    if seam:
                        rt = jnp.where(lane == 63, right[H], rt)
                        lf = jnp.where(lane == 64, left[H], lf)
                else:
                    rt = jnp.where(lane == 63, right[E], right[H])
                    lf = jnp.where(lane == 64, left[E], left[H])
                up = src[t, g, pl.ds(e + 1, 8), :]
                dn = src[t, g, pl.ds(e - 1, 8), :]
                dp, ds = up - dn, rt - lf
                around = (up + dn) + (rt + lf)
                for f in range(F):
                    term = along_pitch[f][g] * dp + along_span[f][g] * ds
                    if f == g:
                        term = term + (keep[g] * here[t] + visc[g] * around)
                    total[t][f] = term if total[t][f] is None else total[t][f] + term
        return total

    def first_step(src, dst, mats, outs, seam, lo, hi):
        @pl.loop(lo, hi)
        def _(b):
            e = pl.multiple_of(b * 8 + PAD, 8)
            total = stencil(src, mats, e, outs, seam)
            for t in outs:
                for f in range(F):
                    value = total[t][f]
                    if t == H:
                        value = jnp.where(inside, value, 0.0)
                    dst[t, f, pl.ds(e, 8), :] = value

    def to_end(outs, lo, hi):
        @pl.loop(lo, hi)
        def _(b):
            e = pl.multiple_of(b * 8 + PAD, 8)
            r = pl.multiple_of(b * 8, 8)
            total = stencil(v1, fwd, e, outs, E in outs)
            for f in range(F):
                both = rotate_in(force[f, pl.ds(r, 8), 0:L], force[f, pl.ds(r, 8), L : 2 * L])
                for t in outs:
                    end[t, f, pl.ds(r, 8), :] = total[t][f] + 0.25 * both[t]

    def stream_a(t, c):
        return pltpu.make_async_remote_copy(
            src_ref=v0.at[t, :, pl.ds(pl.multiple_of(c * CH + PAD, 8), CH)],
            dst_ref=got_a.at[t, :, pl.ds(pl.multiple_of(c * CH, 8), CH)],
            send_sem=a_send.at[t, c], recv_sem=a_recv.at[t, c],
            device_id=along("seg", -1), device_id_type=MESH,
        )

    def stream_b(t, c):
        part = pl.ds(pl.multiple_of(c * CH, 8), CH)
        return pltpu.make_async_remote_copy(
            src_ref=end.at[t, :, part], dst_ref=got_b.at[t, :, part],
            send_sem=b_send.at[t, c], recv_sem=b_recv.at[t, c],
            device_id=along("seg", 1), device_id_type=MESH,
        )

    def columns(phase, side):
        source, target = ((packed, halo), (packed2, halo2))[phase]
        return pltpu.make_async_remote_copy(
            src_ref=source, dst_ref=target.at[side],
            send_sem=col_send.at[phase, side], recv_sem=col_recv.at[phase, side],
            device_id=along("span", (1, -1)[side]), device_id_type=MESH,
        )

    def edge_rows(phase, side):
        field = (v0, w0)[phase]
        if side == 0:
            src, dst = pl.ds(PAD + rows - 8, 8), pl.ds(PAD - 8, 8)
        else:
            src, dst = pl.ds(PAD, 8), pl.ds(PAD + rows, 8)
        return pltpu.make_async_remote_copy(
            src_ref=field.at[:, :, src], dst_ref=field.at[:, :, dst],
            send_sem=row_send.at[phase, side], recv_sem=row_recv.at[phase, side],
            device_id=along("pitch", (1, -1)[side]), device_id_type=MESH,
        )

    def pack(field, out):
        @pl.loop(0, blocks)
        def _(b):
            e = pl.multiple_of(b * 8 + PAD, 8)
            value = field[E, 2, pl.ds(e, 8), :]
            for f in (0, 1, 3, 4):
                at = 54 + 4 * f
                mine = (lane >= at) & (lane < at + 4)
                value = jnp.where(mine, rolled(field[E, f, pl.ds(e, 8), :], 4 * (f - 2)), value)
            out[pl.ds(pl.multiple_of(b * 8, 8), 8), :] = value

    def unpack(arrived, field):
        @pl.loop(0, blocks)
        def _(b):
            e = pl.multiple_of(b * 8 + PAD, 8)
            r = pl.multiple_of(b * 8, 8)
            value = jnp.where(packed_left, arrived[0, pl.ds(r, 8), :], arrived[1, pl.ds(r, 8), :])
            value = jnp.where(packed_inside, value, 0.0)
            for f in range(F):
                field[H, f, pl.ds(e, 8), :] = rolled(value, -4 * (f - 2))

    @pl.loop(0, chunks)
    def _(c):
        load(states, raw, load_s, c).wait()

        @pl.loop(0, CH // 8)
        def _(i):
            r = pl.multiple_of(c * CH + i * 8, 8)
            e = pl.multiple_of(r + PAD, 8)
            for f in range(F):
                mid, edge = rotate_in(raw[f, pl.ds(r, 8), 0:L], raw[f, pl.ds(r, 8), L : 2 * L])
                v0[M, f, pl.ds(e, 8), :] = mid
                v0[E, f, pl.ds(e, 8), :] = edge

    pack(v0, packed)
    pl.semaphore_wait(barrier, 6)
    for side in (0, 1):
        columns(0, side).start()
    for t in (E, M):
        for c in order:
            stream_a(t, c).start()
    for c in range(chunks):
        load(forcing, force, load_f, c).wait()

    per = CH // 8
    first_step(v0, v1, fwd, (M, E), False, per - 1, per + 1)

    @pl.loop(1, chunks - 1)
    def _(c):
        first_step(v0, v1, fwd, (M, E), False, c * per + 1, c * per + per + 1)
        to_end((M,), c * per, c * per + per)
        stream_b(M, c).start()

    for side in (0, 1):
        columns(0, side).wait()
    unpack(halo, v0)
    for side in (0, 1):
        edge_rows(0, side).start()
    first_step(v0, v1, fwd, (E, H), True, per - 1, blocks - per + 1)
    for side in (0, 1):
        edge_rows(0, side).wait()
    first_step(v0, v1, fwd, (M, E, H), True, -1, per - 1)
    first_step(v0, v1, fwd, (M, E, H), True, blocks - per + 1, blocks + 1)
    to_end((M, E), 0, per)
    stream_b(M, 0).start()
    stream_b(E, 0).start()

    @pl.loop(1, chunks - 1)
    def _(c):
        to_end((E,), c * per, c * per + per)
        stream_b(E, c).start()

    to_end((M, E), blocks - per, blocks)
    stream_b(M, chunks - 1).start()
    stream_b(E, chunks - 1).start()

    def arrive(t, c):
        stream_a(t, c).wait_recv()

        @pl.loop(c * per, c * per + per)
        def _(b):
            e = pl.multiple_of(b * 8 + PAD, 8)
            r = pl.multiple_of(b * 8, 8)
            for f in range(F):
                w0[t, f, pl.ds(e, 8), :] = end[t, f, pl.ds(r, 8), :] - got_a[t, f, pl.ds(r, 8), :]

    arrive(E, 0)
    arrive(E, chunks - 1)

    @pl.loop(1, chunks - 1)
    def _(c):
        arrive(E, c)

    pack(w0, packed2)
    for side in (0, 1):
        columns(1, side).start()
    arrive(M, 0)
    arrive(M, chunks - 1)
    for side in (0, 1):
        columns(1, side).wait()
    unpack(halo2, w0)
    for side in (0, 1):
        edge_rows(1, side).start()

    def out_rows(lo, hi):
        @pl.loop(lo, hi)
        def _(b):
            e = pl.multiple_of(b * 8 + PAD, 8)
            r = pl.multiple_of(b * 8, 8)
            for f in range(F):
                one, two = rotate_out(w0[M, f, pl.ds(e, 8), :], w0[E, f, pl.ds(e, 8), :])
                mis_out[0, f, pl.ds(r, 8), 0:L] = one
                mis_out[0, f, pl.ds(r, 8), L : 2 * L] = two

    def adjoint_rows(lo, hi):
        @pl.loop(lo, hi)
        def _(b):
            e = pl.multiple_of(b * 8 + PAD, 8)
            r = pl.multiple_of(b * 8, 8)
            total = stencil(w1, adj, e, (M, E), True)
            for f in range(F):
                parts = [
                    total[t][f] - (got_b[t, f, pl.ds(r, 8), :] - v0[t, f, pl.ds(e, 8), :])
                    for t in (M, E)
                ]
                one, two = rotate_out(*parts)
                grad_out[0, f, pl.ds(r, 8), 0:L] = one
                grad_out[0, f, pl.ds(r, 8), L : 2 * L] = two

    out_rows(0, per)
    out_rows(blocks - per, blocks)
    for side in (0, 1):
        edge_rows(1, side).wait()
    first_step(w0, w1, adj, (M, E, H), True, -1, per - 1)
    stream_b(M, 0).wait_recv()
    stream_b(E, 0).wait_recv()
    adjoint_rows(0, per - 2)

    @pl.loop(1, chunks - 1)
    def _(c):
        arrive(M, c)
        first_step(w0, w1, adj, (M, E, H), True, c * per - 1, c * per + per - 1)
        out_rows(c * per, c * per + per)
        stream_b(M, c).wait_recv()
        stream_b(E, c).wait_recv()
        adjoint_rows(c * per - 2, c * per + per - 2)

    first_step(w0, w1, adj, (M, E, H), True, blocks - per - 1, blocks + 1)
    stream_b(M, chunks - 1).wait_recv()
    stream_b(E, chunks - 1).wait_recv()
    adjoint_rows(blocks - per - 2, blocks)

    for t in (M, E):
        @pl.loop(0, chunks)
        def _(c):
            stream_a(t, c).wait_send()
            stream_b(t, c).wait_send()


def body(states, forcing, adv_pitch, adv_span, diffusion):
    rows = states.shape[2]
    chunks = rows // CH
    tall = rows + 2 * PAD
    shape = jax.ShapeDtypeStruct(states.shape, jnp.float32)
    dma = pltpu.SemaphoreType.DMA
    tiles = pltpu.VMEM((3, F, tall, L), jnp.float32)
    pair = pltpu.VMEM((2, F, rows, L), jnp.float32)
    block = pltpu.VMEM((F, rows, 2 * L), jnp.float32)
    return pl.pallas_call(
        kernel,
        out_shape=(shape, shape),
        in_specs=[pl.BlockSpec(memory_space=pltpu.HBM)] * 2 + [pl.BlockSpec(memory_space=pltpu.SMEM)] * 3,
        out_specs=[pl.BlockSpec(memory_space=pltpu.VMEM)] * 2,
        scratch_shapes=[
            block, block, tiles, tiles, tiles, tiles, pair, pair, pair,
            pltpu.VMEM((rows, L), jnp.float32), pltpu.VMEM((rows, L), jnp.float32),
            pltpu.VMEM((2, rows, L), jnp.float32), pltpu.VMEM((2, rows, L), jnp.float32),
            dma((chunks,)), dma((chunks,)),
            dma((2, chunks)), dma((2, chunks)), dma((2, chunks)), dma((2, chunks)),
            dma((2, 2)), dma((2, 2)), dma((2, 2)), dma((2, 2)),
        ],
        compiler_params=pltpu.CompilerParams(collective_id=0, has_side_effects=True, vmem_limit_bytes=40 << 20),
        name="orbit",
    )(states, forcing, adv_pitch, adv_span, diffusion)


def solution(mesh):
    spread = P("seg", None, "pitch", "span")
    return jax.shard_map(
        body,
        mesh=mesh,
        in_specs=(spread, spread, P(), P(), P()),
        out_specs=(spread, spread),
        check_vma=False,
    )
```

```python
import functools

import jax
import jax.numpy as jnp
from jax import lax
from jax.experimental import pallas as pl
from jax.experimental.pallas import tpu as pltpu
from jax.sharding import PartitionSpec as P

MESH = pl.DeviceIdType.MESH
F = 5
L = 128
PAD = 16
CH = 32
M, E, H = 0, 1, 2


def along(axis, by):
    count = lax.axis_size(axis)
    return {axis: lax.rem(lax.axis_index(axis) + (by + count), count)}


def rolled(x, by):
    return pltpu.roll(x, by % L, 1)


def kernel(
    states, forcing, pitch_ref, span_ref, diff_ref, mis_out, grad_out,
    raw, force, across, v0, v1, w0, w1, end, got_a, got_b, packed, packed2, halo, halo2,
    load_s, load_f, a_send, a_recv, b_send, b_recv, col_send, col_recv, row_send, row_recv,
):
    rows = raw.shape[1]
    chunks = rows // CH
    blocks = rows // 8
    order = [0, chunks - 1] + list(range(1, chunks - 1))

    def load(src, dst, sem, c):
        part = pl.ds(c * CH, CH)
        return pltpu.make_async_copy(src.at[0, :, part], dst.at[:, part], sem.at[c])

    for c in range(chunks):
        load(states, raw, load_s, c).start()
    for c in range(chunks):
        load(forcing, force, load_f, c).start()

    barrier = pltpu.get_barrier_semaphore()
    for axis in ("seg", "pitch", "span"):
        for by in (1, -1):
            pl.semaphore_signal(barrier, inc=1, device_id=along(axis, by), device_id_type=MESH)

    lane = lax.broadcasted_iota(jnp.int32, (8, L), 1)
    low = lane < 64
    span_at, span_of = lax.axis_index("span"), lax.axis_size("span")
    has_left = jnp.where(span_at > 0, 1, 0)
    has_right = jnp.where(span_at < span_of - 1, 1, 0)
    inside = jnp.where(low, has_left, has_right) > 0
    packed_left = (lane & 3) >= 2
    packed_inside = jnp.where(packed_left, has_left, has_right) > 0

    fwd = (
        [[pitch_ref[f, g] * -0.125 for g in range(F)] for f in range(F)],
        [[span_ref[f, g] * -0.125 for g in range(F)] for f in range(F)],
    )
    adj = (
        [[pitch_ref[g, f] * 0.125 for g in range(F)] for f in range(F)],
        [[span_ref[g, f] * 0.125 for g in range(F)] for f in range(F)],
    )
    keep = [1.0 - diff_ref[f] for f in range(F)]
    visc = [diff_ref[f] * 0.25 for f in range(F)]

    def rotate_in(first, second):
        one, two = rolled(first, 64), rolled(second, 64)
        return jnp.where(low, one, two), jnp.where(low, two, one)

    def rotate_out(mid, edge):
        one, two = rolled(mid, 64), rolled(edge, 64)
        return jnp.where(low, two, one), jnp.where(low, one, two)

    def steps(lo, count, run, size=4):
        if count // size:
            @pl.loop(0, count // size)
            def _(i):
                run(lo + i * size, size)
        if count % size:
            run(lo + count // size * size, count % size)

    def row_at(b, pad=PAD):
        return pl.multiple_of(b * 8 + pad, 8)

    def stencil(src, mats, b, n, outs, seam, emit):
        along_pitch, along_span = mats
        for u in range(n):
            part = slice(u * 8, u * 8 + 8)
            for g in range(F):
                right, left = {}, {}
                for t in (M, E, H) if seam else (M, E):
                    here = src[t, g, pl.ds(row_at(b + u), 8), :]
                    right[t] = rolled(here, -1)
                    left[t] = rolled(here, 1)
                for t in outs:
                    if t == M:
                        rt = jnp.where(lane == 127, right[E], right[M])
                        lf = jnp.where(lane == 0, left[E], left[M])
                    elif t == E:
                        rt = jnp.where(lane == 127, right[M], right[E])
                        lf = jnp.where(lane == 0, left[M], left[E])
                        if seam:
                            rt = jnp.where(lane == 63, right[H], rt)
                            lf = jnp.where(lane == 64, left[H], lf)
                    else:
                        rt = jnp.where(lane == 63, right[E], right[H])
                        lf = jnp.where(lane == 64, left[E], left[H])
                    across[0, t, g, part, :] = rt - lf
                    across[1, t, g, part, :] = rt + lf
        for u in range(n):
            e = row_at(b + u)
            part = slice(u * 8, u * 8 + 8)
            total = {t: [None] * F for t in outs}
            for g in range(F):
                for t in outs:
                    up = src[t, g, pl.ds(e + 1, 8), :]
                    dn = src[t, g, pl.ds(e - 1, 8), :]
                    dp, ds = up - dn, across[0, t, g, part, :]
                    around = (up + dn) + across[1, t, g, part, :]
                    for f in range(F):
                        term = along_pitch[f][g] * dp + along_span[f][g] * ds
                        if f == g:
                            term = term + (keep[g] * src[t, g, pl.ds(e, 8), :] + visc[g] * around)
                        total[t][f] = term if total[t][f] is None else total[t][f] + term
            emit(b + u, total)

    def first_step(src, dst, mats, outs, seam, lo, count):
        def emit(b, total):
            for t in outs:
                for f in range(F):
                    value = total[t][f]
                    if t == H:
                        value = jnp.where(inside, value, 0.0)
                    dst[t, f, pl.ds(row_at(b), 8), :] = value

        steps(lo, count, lambda b, n: stencil(src, mats, b, n, outs, seam, emit))

    def to_end(outs, fresh, lo, count):
        def emit(b, total):
            part = pl.ds(row_at(b, 0), 8)
            for f in range(F):
                for t in outs:
                    end[t, f, part, :] = total[t][f] + end[t, f, part, :]

        def run(b, n):
            if fresh:
                for u in range(n):
                    part = pl.ds(row_at(b + u, 0), 8)
                    for f in range(F):
                        both = rotate_in(force[f, part, 0:L], force[f, part, L : 2 * L])
                        end[M, f, part, :] = 0.25 * both[M]
                        end[E, f, part, :] = 0.25 * both[E]
            stencil(v1, fwd, b, n, outs, E in outs, emit)

        steps(lo, count, run)

    def stream_a(t, c):
        return pltpu.make_async_remote_copy(
            src_ref=v0.at[t, :, pl.ds(pl.multiple_of(c * CH + PAD, 8), CH)],
            dst_ref=got_a.at[t, :, pl.ds(pl.multiple_of(c * CH, 8), CH)],
            send_sem=a_send.at[t, c], recv_sem=a_recv.at[t, c],
            device_id=along("seg", -1), device_id_type=MESH,
        )

    def stream_b(t, c):
        part = pl.ds(pl.multiple_of(c * CH, 8), CH)
        return pltpu.make_async_remote_copy(
            src_ref=end.at[t, :, part], dst_ref=got_b.at[t, :, part],
            send_sem=b_send.at[t, c], recv_sem=b_recv.at[t, c],
            device_id=along("seg", 1), device_id_type=MESH,
        )

    def columns(phase, side):
        source, target = ((packed, halo), (packed2, halo2))[phase]
        return pltpu.make_async_remote_copy(
            src_ref=source, dst_ref=target.at[side],
            send_sem=col_send.at[phase, side], recv_sem=col_recv.at[phase, side],
            device_id=along("span", (1, -1)[side]), device_id_type=MESH,
        )

    def edge_rows(phase, side):
        field = (v0, w0)[phase]
        if side == 0:
            src, dst = pl.ds(PAD + rows - 8, 8), pl.ds(PAD - 8, 8)
        else:
            src, dst = pl.ds(PAD, 8), pl.ds(PAD + rows, 8)
        return pltpu.make_async_remote_copy(
            src_ref=field.at[:, :, src], dst_ref=field.at[:, :, dst],
            send_sem=row_send.at[phase, side], recv_sem=row_recv.at[phase, side],
            device_id=along("pitch", (1, -1)[side]), device_id_type=MESH,
        )

    def pack(field, out):
        def run(b, n):
            for u in range(n):
                value = field[E, 2, pl.ds(row_at(b + u), 8), :]
                for f in (0, 1, 3, 4):
                    at = 54 + 4 * f
                    mine = (lane >= at) & (lane < at + 4)
                    value = jnp.where(mine, rolled(field[E, f, pl.ds(row_at(b + u), 8), :], 4 * (f - 2)), value)
                out[pl.ds(row_at(b + u, 0), 8), :] = value

        steps(0, blocks, run, 8)

    def unpack(arrived, field):
        def run(b, n):
            for u in range(n):
                part = pl.ds(row_at(b + u, 0), 8)
                value = jnp.where(packed_left, arrived[0, part, :], arrived[1, part, :])
                value = jnp.where(packed_inside, value, 0.0)
                for f in range(F):
                    field[H, f, pl.ds(row_at(b + u), 8), :] = rolled(value, -4 * (f - 2))

        steps(0, blocks, run, 8)

    per = CH // 8

    @pl.loop(0, chunks)
    def _(c):
        load(states, raw, load_s, c).wait()
        for u in range(per):
            b = c * per + u
            part = pl.ds(row_at(b, 0), 8)
            for f in range(F):
                mid, edge = rotate_in(raw[f, part, 0:L], raw[f, part, L : 2 * L])
                v0[M, f, pl.ds(row_at(b), 8), :] = mid
                v0[E, f, pl.ds(row_at(b), 8), :] = edge

    pack(v0, packed)
    pl.semaphore_wait(barrier, 6)
    for side in (0, 1):
        columns(0, side).start()
    for t in (E, M):
        for c in order:
            stream_a(t, c).start()
    for c in range(chunks):
        load(forcing, force, load_f, c).wait()

    first_step(v0, v1, fwd, (M, E), False, per - 1, 2)

    @pl.loop(1, chunks - 1)
    def _(c):
        first_step(v0, v1, fwd, (M, E), False, c * per + 1, per)
        to_end((M,), True, c * per, per)
        stream_b(M, c).start()

    for side in (0, 1):
        columns(0, side).wait()
    unpack(halo, v0)
    for side in (0, 1):
        edge_rows(0, side).start()
    first_step(v0, v1, fwd, (E, H), True, per - 1, blocks - 2 * per + 2)
    for side in (0, 1):
        edge_rows(0, side).wait()

    @pl.loop(0, 2)
    def _(i):
        first_step(v0, v1, fwd, (M, E, H), True, i * (blocks - per + 2) - 1, per)

    def both_ends(c):
        to_end((M, E), True, c * per, per)
        stream_b(M, c).start()
        stream_b(E, c).start()

    both_ends(0)

    @pl.loop(1, chunks - 1)
    def _(c):
        to_end((E,), False, c * per, per)
        stream_b(E, c).start()

    both_ends(chunks - 1)

    def arrive(t, c):
        stream_a(t, c).wait_recv()

        for u in range(per):
            b = c * per + u
            part = pl.ds(row_at(b, 0), 8)
            for f in range(F):
                w0[t, f, pl.ds(row_at(b), 8), :] = end[t, f, part, :] - got_a[t, f, part, :]

    arrive(E, 0)
    arrive(E, chunks - 1)

    @pl.loop(1, chunks - 1)
    def _(c):
        arrive(E, c)

    pack(w0, packed2)
    for side in (0, 1):
        columns(1, side).start()
    arrive(M, 0)
    arrive(M, chunks - 1)
    for side in (0, 1):
        columns(1, side).wait()
    unpack(halo2, w0)
    for side in (0, 1):
        edge_rows(1, side).start()

    def out_rows(lo, count):
        def run(b, n):
            for u in range(n):
                part = pl.ds(row_at(b + u, 0), 8)
                for f in range(F):
                    one, two = rotate_out(*[w0[t, f, pl.ds(row_at(b + u), 8), :] for t in (M, E)])
                    mis_out[0, f, part, 0:L] = one
                    mis_out[0, f, part, L : 2 * L] = two

        steps(lo, count, run)

    def adjoint_rows(lo, count):
        def emit(b, total):
            part = pl.ds(row_at(b, 0), 8)
            for f in range(F):
                one, two = rotate_out(*[
                    total[t][f] - (got_b[t, f, part, :] - v0[t, f, pl.ds(row_at(b), 8), :]) for t in (M, E)
                ])
                grad_out[0, f, part, 0:L] = one
                grad_out[0, f, part, L : 2 * L] = two

        steps(lo, count, lambda b, n: stencil(w1, adj, b, n, (M, E), True, emit))

    for side in (0, 1):
        edge_rows(1, side).wait()
    first_step(w0, w1, adj, (M, E, H), True, -1, per)
    out_rows(0, per)
    stream_b(M, 0).wait_recv()
    stream_b(E, 0).wait_recv()
    adjoint_rows(0, per - 2)

    @pl.loop(1, chunks - 1)
    def _(c):
        arrive(M, c)
        first_step(w0, w1, adj, (M, E, H), True, c * per - 1, per)
        out_rows(c * per, per)
        stream_b(M, c).wait_recv()
        stream_b(E, c).wait_recv()
        adjoint_rows(c * per - 2, per)

    first_step(w0, w1, adj, (M, E, H), True, blocks - per - 1, per + 2)
    out_rows(blocks - per, per)
    stream_b(M, chunks - 1).wait_recv()
    stream_b(E, chunks - 1).wait_recv()
    adjoint_rows(blocks - per - 2, per + 2)

    for t in (M, E):
        @pl.loop(0, chunks)
        def _(c):
            stream_a(t, c).wait_send()
            stream_b(t, c).wait_send()


def body(states, forcing, adv_pitch, adv_span, diffusion):
    states, forcing, adv_pitch, adv_span, diffusion = (
        pltpu.with_memory_space_constraint(x, pltpu.HBM) for x in (states, forcing, adv_pitch, adv_span, diffusion)
    )
    rows = states.shape[2]
    chunks = rows // CH
    tall = rows + 2 * PAD
    shape = jax.ShapeDtypeStruct(states.shape, jnp.float32)
    dma = pltpu.SemaphoreType.DMA
    tiles = pltpu.VMEM((3, F, tall, L), jnp.float32)
    pair = pltpu.VMEM((2, F, rows, L), jnp.float32)
    block = pltpu.VMEM((F, rows, 2 * L), jnp.float32)
    return pl.pallas_call(
        kernel,
        out_shape=(shape, shape),
        in_specs=[pl.BlockSpec(memory_space=pltpu.HBM)] * 2 + [pl.BlockSpec(memory_space=pltpu.SMEM)] * 3,
        out_specs=[pl.BlockSpec(memory_space=pltpu.VMEM)] * 2,
        scratch_shapes=[
            block, block, pltpu.VMEM((2, 3, F, CH, L), jnp.float32), tiles, tiles, tiles, tiles, pair, pair, pair,
            pltpu.VMEM((rows, L), jnp.float32), pltpu.VMEM((rows, L), jnp.float32),
            pltpu.VMEM((2, rows, L), jnp.float32), pltpu.VMEM((2, rows, L), jnp.float32),
            dma((chunks,)), dma((chunks,)),
            dma((2, chunks)), dma((2, chunks)), dma((2, chunks)), dma((2, chunks)),
            dma((2, 2)), dma((2, 2)), dma((2, 2)), dma((2, 2)),
        ],
        compiler_params=pltpu.CompilerParams(collective_id=0, has_side_effects=True, vmem_limit_bytes=40 << 20),
        name="orbit",
    )(states, forcing, adv_pitch, adv_span, diffusion)


def solution(mesh):
    spread = P("seg", None, "pitch", "span")
    return jax.shard_map(
        body,
        mesh=mesh,
        in_specs=(spread, spread, P(), P(), P()),
        out_specs=(spread, spread),
        check_vma=False,
    )
```

```python
import functools

import jax
import jax.numpy as jnp
from jax import lax
from jax.experimental import pallas as pl
from jax.experimental.pallas import tpu as pltpu
from jax.sharding import PartitionSpec as P

MESH = pl.DeviceIdType.MESH
F = 5
L = 128
PAD = 16
CH = 32
M, E, H = 0, 1, 2


def along(axis, by):
    count = lax.axis_size(axis)
    return {axis: lax.rem(lax.axis_index(axis) + (by + count), count)}


def rolled(x, by):
    return pltpu.roll(x, by % L, 1)


def kernel(
    states, forcing, pitch_hbm, span_hbm, diff_hbm, mis_out, grad_out,
    pitch_ref, span_ref, diff_ref, raw, force, across, v0, v1, w0, w1, end, got_a, got_b, packed, packed2, halo, halo2,
    load_c, load_s, load_f, a_send, a_recv, b_send, b_recv, col_send, col_recv, row_send, row_recv,
):
    rows = raw.shape[1]
    chunks = rows // CH
    blocks = rows // 8
    per = CH // 8
    half = chunks // 2
    outer_first = [c for i in range(half) for c in (i, chunks - 1 - i)]

    def load(src, dst, sem, c):
        part = pl.ds(c * CH, CH)
        return pltpu.make_async_copy(src.at[0, :, part], dst.at[:, part], sem.at[c])

    for c in range(chunks):
        load(states, raw, load_s, c).start()
    coefs = [
        pltpu.make_async_copy(src, dst, load_c.at[i])
        for i, (src, dst) in enumerate(((pitch_hbm, pitch_ref), (span_hbm, span_ref), (diff_hbm, diff_ref)))
    ]
    for copy in coefs:
        copy.start()

    barrier = pltpu.get_barrier_semaphore()
    for axis in ("seg", "pitch", "span"):
        for by in (1, -1):
            pl.semaphore_signal(barrier, inc=1, device_id=along(axis, by), device_id_type=MESH)

    lane = lax.broadcasted_iota(jnp.int32, (8, L), 1)
    low = lane < 64
    span_at, span_of = lax.axis_index("span"), lax.axis_size("span")
    has_left = jnp.where(span_at > 0, 1, 0)
    has_right = jnp.where(span_at < span_of - 1, 1, 0)
    inside = jnp.where(low, has_left, has_right) > 0
    packed_left = (lane & 3) >= 2
    packed_inside = jnp.where(packed_left, has_left, has_right) > 0

    def rotate_in(first, second):
        one, two = rolled(first, 64), rolled(second, 64)
        return jnp.where(low, one, two), jnp.where(low, two, one)

    def rotate_out(mid, edge):
        one, two = rolled(mid, 64), rolled(edge, 64)
        return jnp.where(low, two, one), jnp.where(low, one, two)

    def steps(lo, count, run, size=4):
        if count // size:
            @pl.loop(0, count // size)
            def _(i):
                run(lo + i * size, size)
        if count % size:
            run(lo + count // size * size, count % size)

    def row_at(b, pad=PAD):
        return pl.multiple_of(b * 8 + pad, 8)

    def stencil(src, mats, b, n, outs, seam, emit):
        along_pitch, along_span = mats
        for u in range(n):
            part = slice(u * 8, u * 8 + 8)
            for g in range(F):
                right, left = {}, {}
                for t in (M, E, H) if seam else (M, E):
                    here = src[t, g, pl.ds(row_at(b + u), 8), :]
                    right[t] = rolled(here, -1)
                    left[t] = rolled(here, 1)
                for t in outs:
                    if t == M:
                        rt = jnp.where(lane == 127, right[E], right[M])
                        lf = jnp.where(lane == 0, left[E], left[M])
                    elif t == E:
                        rt = jnp.where(lane == 127, right[M], right[E])
                        lf = jnp.where(lane == 0, left[M], left[E])
                        if seam:
                            rt = jnp.where(lane == 63, right[H], rt)
                            lf = jnp.where(lane == 64, left[H], lf)
                    else:
                        rt = jnp.where(lane == 63, right[E], right[H])
                        lf = jnp.where(lane == 64, left[E], left[H])
                    across[0, t, g, part, :] = rt - lf
                    across[1, t, g, part, :] = rt + lf
        for u in range(n):
            e = row_at(b + u)
            part = slice(u * 8, u * 8 + 8)
            total = {t: [None] * F for t in outs}
            for g in range(F):
                for t in outs:
                    up = src[t, g, pl.ds(e + 1, 8), :]
                    dn = src[t, g, pl.ds(e - 1, 8), :]
                    dp, ds = up - dn, across[0, t, g, part, :]
                    around = (up + dn) + across[1, t, g, part, :]
                    for f in range(F):
                        term = along_pitch[f][g] * dp + along_span[f][g] * ds
                        if f == g:
                            term = term + (keep[g] * src[t, g, pl.ds(e, 8), :] + visc[g] * around)
                        total[t][f] = term if total[t][f] is None else total[t][f] + term
            emit(b + u, total)

    def first_step(src, dst, mats, outs, seam, lo, count):
        def emit(b, total):
            for t in outs:
                for f in range(F):
                    value = total[t][f]
                    if t == H:
                        value = jnp.where(inside, value, 0.0)
                    dst[t, f, pl.ds(row_at(b), 8), :] = value

        steps(lo, count, lambda b, n: stencil(src, mats, b, n, outs, seam, emit))

    def to_end(outs, fresh, lo, count):
        def emit(b, total):
            part = pl.ds(row_at(b, 0), 8)
            for f in range(F):
                for t in outs:
                    end[t, f, part, :] = total[t][f] + end[t, f, part, :]

        def run(b, n):
            if fresh:
                for u in range(n):
                    part = pl.ds(row_at(b + u, 0), 8)
                    for f in range(F):
                        both = rotate_in(force[f, part, 0:L], force[f, part, L : 2 * L])
                        end[M, f, part, :] = 0.25 * both[M]
                        end[E, f, part, :] = 0.25 * both[E]
            stencil(v1, fwd, b, n, outs, E in outs, emit)

        steps(lo, count, run)

    def stream_a(t, c):
        return pltpu.make_async_remote_copy(
            src_ref=v0.at[t, :, pl.ds(pl.multiple_of(c * CH + PAD, 8), CH)],
            dst_ref=got_a.at[t, :, pl.ds(pl.multiple_of(c * CH, 8), CH)],
            send_sem=a_send.at[t, c], recv_sem=a_recv.at[t, c],
            device_id=along("seg", -1), device_id_type=MESH,
        )

    def stream_b(t, c):
        part = pl.ds(pl.multiple_of(c * CH, 8), CH)
        return pltpu.make_async_remote_copy(
            src_ref=end.at[t, :, part], dst_ref=got_b.at[t, :, part],
            send_sem=b_send.at[t, c], recv_sem=b_recv.at[t, c],
            device_id=along("seg", 1), device_id_type=MESH,
        )

    def columns(phase, side):
        source, target = ((packed, halo), (packed2, halo2))[phase]
        return pltpu.make_async_remote_copy(
            src_ref=source, dst_ref=target.at[side],
            send_sem=col_send.at[phase, side], recv_sem=col_recv.at[phase, side],
            device_id=along("span", (1, -1)[side]), device_id_type=MESH,
        )

    def edge_rows(phase, side):
        field = (v0, w0)[phase]
        if side == 0:
            src, dst = pl.ds(PAD + rows - 8, 8), pl.ds(PAD - 8, 8)
        else:
            src, dst = pl.ds(PAD, 8), pl.ds(PAD + rows, 8)
        return pltpu.make_async_remote_copy(
            src_ref=field.at[:, :, src], dst_ref=field.at[:, :, dst],
            send_sem=row_send.at[phase, side], recv_sem=row_recv.at[phase, side],
            device_id=along("pitch", (1, -1)[side]), device_id_type=MESH,
        )

    def pack(field, out):
        def run(b, n):
            for u in range(n):
                value = field[E, 2, pl.ds(row_at(b + u), 8), :]
                for f in (0, 1, 3, 4):
                    at = 54 + 4 * f
                    mine = (lane >= at) & (lane < at + 4)
                    value = jnp.where(mine, rolled(field[E, f, pl.ds(row_at(b + u), 8), :], 4 * (f - 2)), value)
                out[pl.ds(row_at(b + u, 0), 8), :] = value

        steps(0, blocks, run, 8)

    def unpack(arrived, field):
        def run(b, n):
            for u in range(n):
                part = pl.ds(row_at(b + u, 0), 8)
                value = jnp.where(packed_left, arrived[0, part, :], arrived[1, part, :])
                value = jnp.where(packed_inside, value, 0.0)
                for f in range(F):
                    field[H, f, pl.ds(row_at(b + u), 8), :] = rolled(value, -4 * (f - 2))

        steps(0, blocks, run, 8)

    @pl.loop(0, chunks)
    def _(c):
        load(states, raw, load_s, c).wait()
        for u in range(per):
            b = c * per + u
            part = pl.ds(row_at(b, 0), 8)
            for f in range(F):
                mid, edge = rotate_in(raw[f, part, 0:L], raw[f, part, L : 2 * L])
                v0[M, f, pl.ds(row_at(b), 8), :] = mid
                v0[E, f, pl.ds(row_at(b), 8), :] = edge

    for c in range(chunks):
        load(forcing, force, load_f, c).start()
    pl.semaphore_wait(barrier, 6)
    for c in outer_first:
        stream_a(E, c).start()
    pack(v0, packed)
    for side in (0, 1):
        columns(0, side).start()
    for c in outer_first:
        stream_a(M, c).start()
    for copy in coefs:
        copy.wait()
    for c in range(chunks):
        load(forcing, force, load_f, c).wait()

    fwd = (
        [[pitch_ref[f, g] * -0.125 for g in range(F)] for f in range(F)],
        [[span_ref[f, g] * -0.125 for g in range(F)] for f in range(F)],
    )
    adj = (
        [[pitch_ref[g, f] * 0.125 for g in range(F)] for f in range(F)],
        [[span_ref[g, f] * 0.125 for g in range(F)] for f in range(F)],
    )
    keep = [1.0 - diff_ref[f] for f in range(F)]
    visc = [diff_ref[f] * 0.25 for f in range(F)]

    first_step(v0, v1, fwd, (M, E), False, per - 1, 2)

    @pl.loop(1, chunks - 1)
    def _(c):
        first_step(v0, v1, fwd, (M, E), False, c * per + 1, per)
        to_end((M,), True, c * per, per)
        stream_b(M, c).start()

    for side in (0, 1):
        columns(0, side).wait()
    unpack(halo, v0)
    for side in (0, 1):
        edge_rows(0, side).start()
    first_step(v0, v1, fwd, (E, H), True, per - 1, blocks - 2 * per + 2)
    for side in (0, 1):
        edge_rows(0, side).wait()

    @pl.loop(0, 2)
    def _(i):
        first_step(v0, v1, fwd, (M, E, H), True, i * (blocks - per + 2) - 1, per)

    def both_ends(c):
        to_end((M, E), True, c * per, per)
        stream_b(M, c).start()
        stream_b(E, c).start()

    both_ends(0)
    both_ends(chunks - 1)

    def inward(j):
        lower = j % 2
        return 1 + j // 2 + lower * (chunks - 3 - j // 2 * 2), lower

    @pl.loop(0, chunks - 2)
    def _(j):
        c, _ = inward(j)
        to_end((E,), False, c * per, per)
        stream_b(E, c).start()

    def arrive(t, c):
        stream_a(t, c).wait_recv()

        for u in range(per):
            b = c * per + u
            part = pl.ds(row_at(b, 0), 8)
            for f in range(F):
                w0[t, f, pl.ds(row_at(b), 8), :] = end[t, f, part, :] - got_a[t, f, part, :]

    arrive(E, 0)
    arrive(E, chunks - 1)

    @pl.loop(1, chunks - 1)
    def _(c):
        arrive(E, c)

    pack(w0, packed2)
    for side in (0, 1):
        columns(1, side).start()
    arrive(M, 0)
    arrive(M, chunks - 1)
    for side in (0, 1):
        columns(1, side).wait()
    unpack(halo2, w0)
    for side in (0, 1):
        edge_rows(1, side).start()

    def out_rows(lo, count):
        def run(b, n):
            for u in range(n):
                part = pl.ds(row_at(b + u, 0), 8)
                for f in range(F):
                    one, two = rotate_out(*[w0[t, f, pl.ds(row_at(b + u), 8), :] for t in (M, E)])
                    mis_out[0, f, part, 0:L] = one
                    mis_out[0, f, part, L : 2 * L] = two

        steps(lo, count, run)

    def adjoint_rows(lo, count):
        def emit(b, total):
            part = pl.ds(row_at(b, 0), 8)
            for f in range(F):
                one, two = rotate_out(*[
                    total[t][f] - (got_b[t, f, part, :] - v0[t, f, pl.ds(row_at(b), 8), :]) for t in (M, E)
                ])
                grad_out[0, f, part, 0:L] = one
                grad_out[0, f, part, L : 2 * L] = two

        steps(lo, count, lambda b, n: stencil(w1, adj, b, n, (M, E), True, emit))

    for side in (0, 1):
        edge_rows(1, side).wait()
    def arrive_b(c):
        stream_b(M, c).wait_recv()
        stream_b(E, c).wait_recv()

    @pl.loop(0, 2)
    def _(i):
        first_step(w0, w1, adj, (M, E, H), True, i * (blocks - per + 2) - 1, per)
        out_rows(i * (blocks - per), per)
        arrive_b(i * (chunks - 1))
        adjoint_rows(i * (blocks - per + 2), per - 2)

    @pl.loop(0, chunks - 3)
    def _(j):
        c, lower = inward(j)
        arrive(M, c)
        first_step(w0, w1, adj, (M, E, H), True, c * per - 1 + 2 * lower, per)
        out_rows(c * per, per)
        arrive_b(c)
        adjoint_rows(c * per - 2 + 4 * lower, per)

    arrive(M, half)
    first_step(w0, w1, adj, (M, E, H), True, half * per - 1, per + 2)
    out_rows(half * per, per)

    def keep_adjoint(b, total):
        for f in range(F):
            for t in (M, E):
                w0[t, f, pl.ds(row_at(b), 8), :] = total[t][f]

    steps(half * per - 2, per + 4, lambda b, n: stencil(w1, adj, b, n, (M, E), True, keep_adjoint))
    arrive_b(half)

    def last_rows(b, n):
        for u in range(n):
            part = pl.ds(row_at(b + u, 0), 8)
            tall = pl.ds(row_at(b + u), 8)
            for f in range(F):
                one, two = rotate_out(*[
                    w0[t, f, tall, :] - (got_b[t, f, part, :] - v0[t, f, tall, :]) for t in (M, E)
                ])
                grad_out[0, f, part, 0:L] = one
                grad_out[0, f, part, L : 2 * L] = two

    steps(half * per - 2, per + 4, last_rows)

    for t in (M, E):
        @pl.loop(0, chunks)
        def _(c):
            stream_a(t, c).wait_send()
            stream_b(t, c).wait_send()


def body(states, forcing, adv_pitch, adv_span, diffusion):
    states, forcing, adv_pitch, adv_span, diffusion = (
        pltpu.with_memory_space_constraint(x, pltpu.HBM) for x in (states, forcing, adv_pitch, adv_span, diffusion)
    )
    rows = states.shape[2]
    chunks = rows // CH
    tall = rows + 2 * PAD
    shape = jax.ShapeDtypeStruct(states.shape, jnp.float32)
    dma = pltpu.SemaphoreType.DMA
    tiles = pltpu.VMEM((3, F, tall, L), jnp.float32)
    pair = pltpu.VMEM((2, F, rows, L), jnp.float32)
    block = pltpu.VMEM((F, rows, 2 * L), jnp.float32)
    return pl.pallas_call(
        kernel,
        out_shape=(shape, shape),
        in_specs=[pl.BlockSpec(memory_space=pltpu.HBM)] * 5,
        out_specs=[pl.BlockSpec(memory_space=pltpu.VMEM)] * 2,
        scratch_shapes=[
            pltpu.SMEM((F, F), jnp.float32), pltpu.SMEM((F, F), jnp.float32), pltpu.SMEM((F,), jnp.float32),
            block, block, pltpu.VMEM((2, 3, F, CH, L), jnp.float32), tiles, tiles, tiles, tiles, pair, pair, pair,
            pltpu.VMEM((rows, L), jnp.float32), pltpu.VMEM((rows, L), jnp.float32),
            pltpu.VMEM((2, rows, L), jnp.float32), pltpu.VMEM((2, rows, L), jnp.float32),
            dma((3,)), dma((chunks,)), dma((chunks,)),
            dma((2, chunks)), dma((2, chunks)), dma((2, chunks)), dma((2, chunks)),
            dma((2, 2)), dma((2, 2)), dma((2, 2)), dma((2, 2)),
        ],
        compiler_params=pltpu.CompilerParams(collective_id=0, has_side_effects=True, vmem_limit_bytes=40 << 20),
        name="orbit",
    )(states, forcing, adv_pitch, adv_span, diffusion)


def solution(mesh):
    spread = P("seg", None, "pitch", "span")
    return jax.shard_map(
        body,
        mesh=mesh,
        in_specs=(spread, spread, P(), P(), P()),
        out_specs=(spread, spread),
        check_vma=False,
    )
```

```python
import functools

import jax
import jax.numpy as jnp
from jax import lax
from jax.experimental import pallas as pl
from jax.experimental.pallas import tpu as pltpu
from jax.sharding import PartitionSpec as P

MESH = pl.DeviceIdType.MESH
F = 5
L = 128
PAD = 16
CH = 32
M, E, H = 0, 1, 2


def along(axis, by):
    count = lax.axis_size(axis)
    return {axis: lax.rem(lax.axis_index(axis) + (by + count), count)}


def rolled(x, by):
    return pltpu.roll(x, by % L, 1)


def kernel(
    states, forcing, pitch_hbm, span_hbm, diff_hbm, mis_out, grad_out,
    pitch_ref, span_ref, diff_ref, raw, force, across, v0, v1, w0, w1, end, got_a, got_b, packed, packed2, halo, halo2,
    load_c, load_s, load_f, a_send, a_recv, b_send, b_recv, col_send, col_recv, pair_send, pair_recv, row_send, row_recv,
):
    rows = raw.shape[1]
    chunks = rows // CH
    assert chunks == 8
    blocks = rows // 8
    per = CH // 8
    half = chunks // 2
    outer_first = [c for i in range(half) for c in (i, chunks - 1 - i)]
    a_order = [(t, c) for part in (outer_first[:2], outer_first[2:]) for t in (E, M) for c in part]

    def load(src, dst, sem, c):
        part = pl.ds(c * CH, CH)
        return pltpu.make_async_copy(src.at[0, :, part], dst.at[:, part], sem.at[c])

    for c in range(chunks):
        load(states, raw, load_s, c).start()
    coefs = [
        pltpu.make_async_copy(src, dst, load_c.at[i])
        for i, (src, dst) in enumerate(((pitch_hbm, pitch_ref), (span_hbm, span_ref), (diff_hbm, diff_ref)))
    ]
    for copy in coefs:
        copy.start()

    barrier = pltpu.get_barrier_semaphore()
    for axis in ("seg", "pitch", "span"):
        for by in (1, -1):
            pl.semaphore_signal(barrier, inc=1, device_id=along(axis, by), device_id_type=MESH)

    lane = lax.broadcasted_iota(jnp.int32, (8, L), 1)
    low = lane < 64
    span_at, span_of = lax.axis_index("span"), lax.axis_size("span")
    has_left = jnp.where(span_at > 0, 1, 0)
    has_right = jnp.where(span_at < span_of - 1, 1, 0)
    inside = jnp.where(low, has_left, has_right) > 0
    packed_left = (lane & 3) >= 2
    packed_inside = jnp.where(packed_left, has_left, has_right) > 0

    def rotate_in(first, second):
        one, two = rolled(first, 64), rolled(second, 64)
        return jnp.where(low, one, two), jnp.where(low, two, one)

    def rotate_out(mid, edge):
        one, two = rolled(mid, 64), rolled(edge, 64)
        return jnp.where(low, two, one), jnp.where(low, one, two)

    def steps(lo, count, run, size=4):
        if count // size:
            @pl.loop(0, count // size)
            def _(i):
                run(lo + i * size, size)
        if count % size:
            run(lo + count // size * size, count % size)

    def row_at(b, pad=PAD):
        return pl.multiple_of(b * 8 + pad, 8)

    def stencil(src, mats, b, n, outs, seam, emit):
        along_pitch, along_span = mats
        for u in range(n):
            part = slice(u * 8, u * 8 + 8)
            for g in range(F):
                right, left = {}, {}
                for t in (M, E, H) if seam else (M, E):
                    here = src[t, g, pl.ds(row_at(b + u), 8), :]
                    right[t] = rolled(here, -1)
                    left[t] = rolled(here, 1)
                for t in outs:
                    if t == M:
                        rt = jnp.where(lane == 127, right[E], right[M])
                        lf = jnp.where(lane == 0, left[E], left[M])
                    elif t == E:
                        rt = jnp.where(lane == 127, right[M], right[E])
                        lf = jnp.where(lane == 0, left[M], left[E])
                        if seam:
                            rt = jnp.where(lane == 63, right[H], rt)
                            lf = jnp.where(lane == 64, left[H], lf)
                    else:
                        rt = jnp.where(lane == 63, right[E], right[H])
                        lf = jnp.where(lane == 64, left[E], left[H])
                    across[0, t, g, part, :] = rt - lf
                    across[1, t, g, part, :] = rt + lf
        for u in range(n):
            e = row_at(b + u)
            part = slice(u * 8, u * 8 + 8)
            total = {t: [None] * F for t in outs}
            for g in range(F):
                for t in outs:
                    up = src[t, g, pl.ds(e + 1, 8), :]
                    dn = src[t, g, pl.ds(e - 1, 8), :]
                    dp, ds = up - dn, across[0, t, g, part, :]
                    around = (up + dn) + across[1, t, g, part, :]
                    for f in range(F):
                        term = along_pitch[f][g] * dp + along_span[f][g] * ds
                        if f == g:
                            term = term + (keep[g] * src[t, g, pl.ds(e, 8), :] + visc[g] * around)
                        total[t][f] = term if total[t][f] is None else total[t][f] + term
            emit(b + u, total)

    def first_step(src, dst, mats, outs, seam, lo, count):
        def emit(b, total):
            for t in outs:
                for f in range(F):
                    value = total[t][f]
                    if t == H:
                        value = jnp.where(inside, value, 0.0)
                    dst[t, f, pl.ds(row_at(b), 8), :] = value

        steps(lo, count, lambda b, n: stencil(src, mats, b, n, outs, seam, emit))

    def to_end(outs, fresh, lo, count):
        def emit(b, total):
            part = pl.ds(row_at(b, 0), 8)
            for f in range(F):
                for t in outs:
                    end[t, f, part, :] = total[t][f] + end[t, f, part, :]

        def run(b, n):
            if fresh:
                for u in range(n):
                    part = pl.ds(row_at(b + u, 0), 8)
                    for f in range(F):
                        both = rotate_in(force[f, part, 0:L], force[f, part, L : 2 * L])
                        end[M, f, part, :] = 0.25 * both[M]
                        end[E, f, part, :] = 0.25 * both[E]
            stencil(v1, fwd, b, n, outs, E in outs, emit)

        steps(lo, count, run)

    def stream_a(t, c):
        return pltpu.make_async_remote_copy(
            src_ref=v0.at[t, :, pl.ds(pl.multiple_of(c * CH + PAD, 8), CH)],
            dst_ref=got_a.at[t, :, pl.ds(pl.multiple_of(c * CH, 8), CH)],
            send_sem=a_send.at[t, c], recv_sem=a_recv.at[t, c],
            device_id=along("seg", -1), device_id_type=MESH,
        )

    def stream_b(t, c):
        part = pl.ds(pl.multiple_of(c * CH, 8), CH)
        return pltpu.make_async_remote_copy(
            src_ref=end.at[t, :, part], dst_ref=got_b.at[t, :, part],
            send_sem=b_send.at[t, c], recv_sem=b_recv.at[t, c],
            device_id=along("seg", 1), device_id_type=MESH,
        )

    def columns(side):
        return pltpu.make_async_remote_copy(
            src_ref=packed, dst_ref=halo.at[side],
            send_sem=col_send.at[side], recv_sem=col_recv.at[side],
            device_id=along("span", (1, -1)[side]), device_id_type=MESH,
        )

    def pair_columns(k, side):
        return pltpu.make_async_remote_copy(
            src_ref=packed2.at[k], dst_ref=halo2.at[side, k],
            send_sem=pair_send.at[k, side], recv_sem=pair_recv.at[k, side],
            device_id=along("span", (1, -1)[side]), device_id_type=MESH,
        )

    def edge_rows(phase, side):
        field = (v0, w0)[phase]
        if side == 0:
            src, dst = pl.ds(PAD + rows - 8, 8), pl.ds(PAD - 8, 8)
        else:
            src, dst = pl.ds(PAD, 8), pl.ds(PAD + rows, 8)
        return pltpu.make_async_remote_copy(
            src_ref=field.at[:, :, src], dst_ref=field.at[:, :, dst],
            send_sem=row_send.at[phase, side], recv_sem=row_recv.at[phase, side],
            device_id=along("pitch", (1, -1)[side]), device_id_type=MESH,
        )

    def pack_block(field, b):
        value = field[E, 2, pl.ds(row_at(b), 8), :]
        for f in (0, 1, 3, 4):
            at = 54 + 4 * f
            mine = (lane >= at) & (lane < at + 4)
            value = jnp.where(mine, rolled(field[E, f, pl.ds(row_at(b), 8), :], 4 * (f - 2)), value)
        return value

    def unpack_block(from_left, from_right, field, b):
        value = jnp.where(packed_left, from_left, from_right)
        value = jnp.where(packed_inside, value, 0.0)
        for f in range(F):
            field[H, f, pl.ds(row_at(b), 8), :] = rolled(value, -4 * (f - 2))

    def pack_all(b, n):
        for u in range(n):
            packed[pl.ds(row_at(b + u, 0), 8), :] = pack_block(v0, b + u)

    def unpack_all(b, n):
        for u in range(n):
            part = pl.ds(row_at(b + u, 0), 8)
            unpack_block(halo[0, part, :], halo[1, part, :], v0, b + u)

    def pair_blocks(k):
        return [(c * per + u, slice(i * CH + u * 8, i * CH + u * 8 + 8))
                for i, c in enumerate((k, chunks - 1 - k)) for u in range(per)]

    def send_pair(k):
        arrive(E, k)
        arrive(E, chunks - 1 - k)
        for b, part in pair_blocks(k):
            packed2[k, part, :] = pack_block(w0, b)
        for side in (0, 1):
            pair_columns(k, side).start()

    def take_pair(k):
        for side in (0, 1):
            pair_columns(k, side).wait()
        for b, part in pair_blocks(k):
            unpack_block(halo2[0, k, part, :], halo2[1, k, part, :], w0, b)

    @pl.loop(0, chunks)
    def _(c):
        load(states, raw, load_s, c).wait()
        for u in range(per):
            b = c * per + u
            part = pl.ds(row_at(b, 0), 8)
            for f in range(F):
                mid, edge = rotate_in(raw[f, part, 0:L], raw[f, part, L : 2 * L])
                v0[M, f, pl.ds(row_at(b), 8), :] = mid
                v0[E, f, pl.ds(row_at(b), 8), :] = edge

    for c in range(chunks):
        load(forcing, force, load_f, c).start()
    pl.semaphore_wait(barrier, 6)
    for t, c in a_order:
        stream_a(t, c).start()
    for copy in coefs:
        copy.wait()
    for c in range(chunks):
        load(forcing, force, load_f, c).wait()

    fwd = (
        [[pitch_ref[f, g] * -0.125 for g in range(F)] for f in range(F)],
        [[span_ref[f, g] * -0.125 for g in range(F)] for f in range(F)],
    )
    adj = (
        [[pitch_ref[g, f] * 0.125 for g in range(F)] for f in range(F)],
        [[span_ref[g, f] * 0.125 for g in range(F)] for f in range(F)],
    )
    keep = [1.0 - diff_ref[f] for f in range(F)]
    visc = [diff_ref[f] * 0.25 for f in range(F)]

    def no_halo(c):
        first_step(v0, v1, fwd, (M, E), False, c * per + 1, per)
        to_end((M,), True, c * per, per)
        stream_b(M, c).start()

    first_step(v0, v1, fwd, (M, E), False, per - 1, 2)
    no_halo(1)
    steps(0, blocks, pack_all, 8)
    for side in (0, 1):
        columns(side).start()

    @pl.loop(2, chunks - 1)
    def _(c):
        no_halo(c)

    for side in (0, 1):
        columns(side).wait()
    steps(0, blocks, unpack_all, 8)
    for side in (0, 1):
        edge_rows(0, side).start()
    first_step(v0, v1, fwd, (E, H), True, per - 1, blocks - 2 * per + 2)
    for side in (0, 1):
        edge_rows(0, side).wait()

    @pl.loop(0, 2)
    def _(i):
        first_step(v0, v1, fwd, (M, E, H), True, i * (blocks - per + 2) - 1, per)

    def both_ends(c):
        to_end((M, E), True, c * per, per)
        stream_b(M, c).start()
        stream_b(E, c).start()

    both_ends(0)
    both_ends(chunks - 1)

    def inward(j):
        lower = j % 2
        return 1 + j // 2 + lower * (chunks - 3 - j // 2 * 2), lower

    @pl.loop(0, chunks - 2)
    def _(j):
        c, _ = inward(j)
        to_end((E,), False, c * per, per)
        stream_b(E, c).start()

    def arrive(t, c):
        stream_a(t, c).wait_recv()

        for u in range(per):
            b = c * per + u
            part = pl.ds(row_at(b, 0), 8)
            for f in range(F):
                w0[t, f, pl.ds(row_at(b), 8), :] = end[t, f, part, :] - got_a[t, f, part, :]

    def out_rows(lo, count):
        def run(b, n):
            for u in range(n):
                part = pl.ds(row_at(b + u, 0), 8)
                for f in range(F):
                    one, two = rotate_out(*[w0[t, f, pl.ds(row_at(b + u), 8), :] for t in (M, E)])
                    mis_out[0, f, part, 0:L] = one
                    mis_out[0, f, part, L : 2 * L] = two

        steps(lo, count, run)

    def adjoint_rows(lo, count):
        def emit(b, total):
            part = pl.ds(row_at(b, 0), 8)
            for f in range(F):
                one, two = rotate_out(*[
                    total[t][f] - (got_b[t, f, part, :] - v0[t, f, pl.ds(row_at(b), 8), :]) for t in (M, E)
                ])
                grad_out[0, f, part, 0:L] = one
                grad_out[0, f, part, L : 2 * L] = two

        steps(lo, count, lambda b, n: stencil(w1, adj, b, n, (M, E), True, emit))

    send_pair(0)
    arrive(M, 0)
    arrive(M, chunks - 1)
    send_pair(1)
    take_pair(0)
    for side in (0, 1):
        edge_rows(1, side).start()
    send_pair(2)
    take_pair(1)
    for side in (0, 1):
        edge_rows(1, side).wait()
    send_pair(3)
    take_pair(2)

    def arrive_b(c):
        stream_b(M, c).wait_recv()
        stream_b(E, c).wait_recv()

    @pl.loop(0, 2)
    def _(i):
        first_step(w0, w1, adj, (M, E, H), True, i * (blocks - per + 2) - 1, per)
        out_rows(i * (blocks - per), per)
        arrive_b(i * (chunks - 1))
        adjoint_rows(i * (blocks - per + 2), per - 2)

    def inner_step(j):
        c, lower = inward(j)
        arrive(M, c)
        first_step(w0, w1, adj, (M, E, H), True, c * per - 1 + 2 * lower, per)
        out_rows(c * per, per)
        arrive_b(c)
        adjoint_rows(c * per - 2 + 4 * lower, per)

    pl.loop(0, 2)(inner_step)
    take_pair(3)
    pl.loop(2, chunks - 3)(inner_step)

    arrive(M, half)
    first_step(w0, w1, adj, (M, E, H), True, half * per - 1, per + 2)
    out_rows(half * per, per)

    def keep_adjoint(b, total):
        for f in range(F):
            for t in (M, E):
                w0[t, f, pl.ds(row_at(b), 8), :] = total[t][f]

    steps(half * per - 2, per + 4, lambda b, n: stencil(w1, adj, b, n, (M, E), True, keep_adjoint))
    arrive_b(half)

    def last_rows(b, n):
        for u in range(n):
            part = pl.ds(row_at(b + u, 0), 8)
            tall = pl.ds(row_at(b + u), 8)
            for f in range(F):
                one, two = rotate_out(*[
                    w0[t, f, tall, :] - (got_b[t, f, part, :] - v0[t, f, tall, :]) for t in (M, E)
                ])
                grad_out[0, f, part, 0:L] = one
                grad_out[0, f, part, L : 2 * L] = two

    steps(half * per - 2, per + 4, last_rows)

    for t in (M, E):
        @pl.loop(0, chunks)
        def _(c):
            stream_a(t, c).wait_send()
            stream_b(t, c).wait_send()


def body(states, forcing, adv_pitch, adv_span, diffusion):
    states, forcing, adv_pitch, adv_span, diffusion = (
        pltpu.with_memory_space_constraint(x, pltpu.HBM) for x in (states, forcing, adv_pitch, adv_span, diffusion)
    )
    rows = states.shape[2]
    chunks = rows // CH
    tall = rows + 2 * PAD
    shape = jax.ShapeDtypeStruct(states.shape, jnp.float32)
    dma = pltpu.SemaphoreType.DMA
    tiles = pltpu.VMEM((3, F, tall, L), jnp.float32)
    pair = pltpu.VMEM((2, F, rows, L), jnp.float32)
    block = pltpu.VMEM((F, rows, 2 * L), jnp.float32)
    return pl.pallas_call(
        kernel,
        out_shape=(shape, shape),
        in_specs=[pl.BlockSpec(memory_space=pltpu.HBM)] * 5,
        out_specs=[pl.BlockSpec(memory_space=pltpu.VMEM)] * 2,
        scratch_shapes=[
            pltpu.SMEM((F, F), jnp.float32), pltpu.SMEM((F, F), jnp.float32), pltpu.SMEM((F,), jnp.float32),
            block, block, pltpu.VMEM((2, 3, F, CH, L), jnp.float32), tiles, tiles, tiles, tiles, pair, pair, pair,
            pltpu.VMEM((rows, L), jnp.float32), pltpu.VMEM((chunks // 2, 2 * CH, L), jnp.float32),
            pltpu.VMEM((2, rows, L), jnp.float32), pltpu.VMEM((2, chunks // 2, 2 * CH, L), jnp.float32),
            dma((3,)), dma((chunks,)), dma((chunks,)),
            dma((2, chunks)), dma((2, chunks)), dma((2, chunks)), dma((2, chunks)),
            dma((2,)), dma((2,)), dma((chunks // 2, 2)), dma((chunks // 2, 2)), dma((2, 2)), dma((2, 2)),
        ],
        compiler_params=pltpu.CompilerParams(collective_id=0, has_side_effects=True, vmem_limit_bytes=40 << 20),
        name="orbit",
    )(states, forcing, adv_pitch, adv_span, diffusion)


def solution(mesh):
    spread = P("seg", None, "pitch", "span")
    return jax.shard_map(
        body,
        mesh=mesh,
        in_specs=(spread, spread, P(), P(), P()),
        out_specs=(spread, spread),
        check_vma=False,
    )
```

```python
import functools

import jax
import jax.numpy as jnp
from jax import lax
from jax.experimental import pallas as pl
from jax.experimental.pallas import tpu as pltpu
from jax.sharding import PartitionSpec as P

MESH = pl.DeviceIdType.MESH
F = 5
L = 128
PAD = 16
CH = 32
M, E, H = 0, 1, 2


def along(axis, by):
    count = lax.axis_size(axis)
    return {axis: lax.rem(lax.axis_index(axis) + (by + count), count)}


def rolled(x, by):
    return pltpu.roll(x, by % L, 1)


def kernel(
    states, forcing, pitch_hbm, span_hbm, diff_hbm, mis_out, grad_out,
    pitch_ref, span_ref, diff_ref, raw, force, across, v0, v1, w0, w1, end, got_a, got_b, packed, packed2, halo, halo2,
    load_c, load_s, load_f, a_send, a_recv, b_send, b_recv, col_send, col_recv, pair_send, pair_recv, row_send, row_recv,
):
    rows = raw.shape[1]
    chunks = rows // CH
    assert chunks == 8
    blocks = rows // 8
    per = CH // 8
    half = chunks // 2
    outer_first = [c for i in range(half) for c in (i, chunks - 1 - i)]
    a_order = [(t, c) for part in (outer_first[:2], outer_first[2:]) for t in (E, M) for c in part]

    def load(src, dst, sem, c):
        part = pl.ds(c * CH, CH)
        return pltpu.make_async_copy(src.at[0, :, part], dst.at[:, part], sem.at[c])

    for c in range(chunks):
        load(states, raw, load_s, c).start()
    coefs = [
        pltpu.make_async_copy(src, dst, load_c.at[i])
        for i, (src, dst) in enumerate(((pitch_hbm, pitch_ref), (span_hbm, span_ref), (diff_hbm, diff_ref)))
    ]
    for copy in coefs:
        copy.start()

    barrier = pltpu.get_barrier_semaphore()
    for axis in ("seg", "pitch", "span"):
        for by in (1, -1):
            pl.semaphore_signal(barrier, inc=1, device_id=along(axis, by), device_id_type=MESH)

    lane = lax.broadcasted_iota(jnp.int32, (8, L), 1)
    low = lane < 64
    span_at, span_of = lax.axis_index("span"), lax.axis_size("span")
    has_left = jnp.where(span_at > 0, 1, 0)
    has_right = jnp.where(span_at < span_of - 1, 1, 0)
    inside = jnp.where(low, has_left, has_right) > 0
    packed_left = (lane & 3) >= 2
    packed_inside = jnp.where(packed_left, has_left, has_right) > 0

    def rotate_in(first, second):
        one, two = rolled(first, 64), rolled(second, 64)
        return jnp.where(low, one, two), jnp.where(low, two, one)

    def rotate_out(mid, edge):
        one, two = rolled(mid, 64), rolled(edge, 64)
        return jnp.where(low, two, one), jnp.where(low, one, two)

    def steps(lo, count, run, size=4):
        if count // size:
            @pl.loop(0, count // size)
            def _(i):
                run(lo + i * size, size)
        if count % size:
            run(lo + count // size * size, count % size)

    def row_at(b, pad=PAD):
        return pl.multiple_of(b * 8 + pad, 8)

    def stencil(src, mats, b, n, outs, seam, emit):
        along_pitch, along_span = mats
        for u in range(n):
            part = slice(u * 8, u * 8 + 8)
            for g in range(F):
                right, left = {}, {}
                for t in (M, E, H) if seam else (M, E):
                    here = src[t, g, pl.ds(row_at(b + u), 8), :]
                    right[t] = rolled(here, -1)
                    left[t] = rolled(here, 1)
                for t in outs:
                    if t == M:
                        rt = jnp.where(lane == 127, right[E], right[M])
                        lf = jnp.where(lane == 0, left[E], left[M])
                    elif t == E:
                        rt = jnp.where(lane == 127, right[M], right[E])
                        lf = jnp.where(lane == 0, left[M], left[E])
                        if seam:
                            rt = jnp.where(lane == 63, right[H], rt)
                            lf = jnp.where(lane == 64, left[H], lf)
                    else:
                        rt = jnp.where(lane == 63, right[E], right[H])
                        lf = jnp.where(lane == 64, left[E], left[H])
                    across[0, t, g, part, :] = rt - lf
                    across[1, t, g, part, :] = rt + lf
        for u in range(n):
            e = row_at(b + u)
            part = slice(u * 8, u * 8 + 8)
            total = {t: [None] * F for t in outs}
            for g in range(F):
                for t in outs:
                    up = src[t, g, pl.ds(e + 1, 8), :]
                    dn = src[t, g, pl.ds(e - 1, 8), :]
                    dp, ds = up - dn, across[0, t, g, part, :]
                    around = (up + dn) + across[1, t, g, part, :]
                    for f in range(F):
                        term = along_pitch[f][g] * dp + along_span[f][g] * ds
                        if f == g:
                            term = term + (keep[g] * src[t, g, pl.ds(e, 8), :] + visc[g] * around)
                        total[t][f] = term if total[t][f] is None else total[t][f] + term
            emit(b + u, total)

    def first_step(src, dst, mats, outs, seam, lo, count):
        def emit(b, total):
            for t in outs:
                for f in range(F):
                    value = total[t][f]
                    if t == H:
                        value = jnp.where(inside, value, 0.0)
                    dst[t, f, pl.ds(row_at(b), 8), :] = value

        steps(lo, count, lambda b, n: stencil(src, mats, b, n, outs, seam, emit))

    def to_end(outs, fresh, lo, count):
        def emit(b, total):
            part = pl.ds(row_at(b, 0), 8)
            for f in range(F):
                for t in outs:
                    end[t, f, part, :] = total[t][f] + end[t, f, part, :]

        def run(b, n):
            if fresh:
                for u in range(n):
                    part = pl.ds(row_at(b + u, 0), 8)
                    for f in range(F):
                        both = rotate_in(force[f, part, 0:L], force[f, part, L : 2 * L])
                        end[M, f, part, :] = 0.25 * both[M]
                        end[E, f, part, :] = 0.25 * both[E]
            stencil(v1, fwd, b, n, outs, E in outs, emit)

        steps(lo, count, run)

    def stream_a(t, c):
        return pltpu.make_async_remote_copy(
            src_ref=v0.at[t, :, pl.ds(pl.multiple_of(c * CH + PAD, 8), CH)],
            dst_ref=got_a.at[t, :, pl.ds(pl.multiple_of(c * CH, 8), CH)],
            send_sem=a_send.at[t, c], recv_sem=a_recv.at[t, c],
            device_id=along("seg", -1), device_id_type=MESH,
        )

    def stream_b(t, c):
        part = pl.ds(pl.multiple_of(c * CH, 8), CH)
        return pltpu.make_async_remote_copy(
            src_ref=end.at[t, :, part], dst_ref=got_b.at[t, :, part],
            send_sem=b_send.at[t, c], recv_sem=b_recv.at[t, c],
            device_id=along("seg", 1), device_id_type=MESH,
        )

    def columns(side):
        return pltpu.make_async_remote_copy(
            src_ref=packed, dst_ref=halo.at[side],
            send_sem=col_send.at[side], recv_sem=col_recv.at[side],
            device_id=along("span", (1, -1)[side]), device_id_type=MESH,
        )

    def pair_columns(k, side):
        return pltpu.make_async_remote_copy(
            src_ref=packed2.at[k], dst_ref=halo2.at[side, k],
            send_sem=pair_send.at[k, side], recv_sem=pair_recv.at[k, side],
            device_id=along("span", (1, -1)[side]), device_id_type=MESH,
        )

    def edge_rows(phase, side):
        field = (v0, w0)[phase]
        if side == 0:
            src, dst = pl.ds(PAD + rows - 8, 8), pl.ds(PAD - 8, 8)
        else:
            src, dst = pl.ds(PAD, 8), pl.ds(PAD + rows, 8)
        return pltpu.make_async_remote_copy(
            src_ref=field.at[:, :, src], dst_ref=field.at[:, :, dst],
            send_sem=row_send.at[phase, side], recv_sem=row_recv.at[phase, side],
            device_id=along("pitch", (1, -1)[side]), device_id_type=MESH,
        )

    def pack_block(field, b):
        value = field[E, 2, pl.ds(row_at(b), 8), :]
        for f in (0, 1, 3, 4):
            at = 54 + 4 * f
            mine = (lane >= at) & (lane < at + 4)
            value = jnp.where(mine, rolled(field[E, f, pl.ds(row_at(b), 8), :], 4 * (f - 2)), value)
        return value

    def unpack_block(from_left, from_right, field, b):
        value = jnp.where(packed_left, from_left, from_right)
        value = jnp.where(packed_inside, value, 0.0)
        for f in range(F):
            field[H, f, pl.ds(row_at(b), 8), :] = rolled(value, -4 * (f - 2))

    def pack_all(b, n):
        for u in range(n):
            packed[pl.ds(row_at(b + u, 0), 8), :] = pack_block(v0, b + u)

    def unpack_all(b, n):
        for u in range(n):
            part = pl.ds(row_at(b + u, 0), 8)
            unpack_block(halo[0, part, :], halo[1, part, :], v0, b + u)

    def pair_blocks(k):
        return [(c * per + u, slice(i * CH + u * 8, i * CH + u * 8 + 8))
                for i, c in enumerate((k, chunks - 1 - k)) for u in range(per)]

    def send_pair(k):
        arrive(E, k)
        arrive(E, chunks - 1 - k)
        for b, part in pair_blocks(k):
            packed2[k, part, :] = pack_block(w0, b)
        for side in (0, 1):
            pair_columns(k, side).start()

    def take_pair(k):
        for side in (0, 1):
            pair_columns(k, side).wait()
        for b, part in pair_blocks(k):
            unpack_block(halo2[0, k, part, :], halo2[1, k, part, :], w0, b)

    @pl.loop(0, chunks)
    def _(c):
        load(states, raw, load_s, c).wait()
        for u in range(per):
            b = c * per + u
            part = pl.ds(row_at(b, 0), 8)
            for f in range(F):
                mid, edge = rotate_in(raw[f, part, 0:L], raw[f, part, L : 2 * L])
                v0[M, f, pl.ds(row_at(b), 8), :] = mid
                v0[E, f, pl.ds(row_at(b), 8), :] = edge

    for c in range(chunks):
        load(forcing, force, load_f, c).start()
    pl.semaphore_wait(barrier, 6)
    for t, c in a_order:
        stream_a(t, c).start()
    for copy in coefs:
        copy.wait()
    for c in range(chunks):
        load(forcing, force, load_f, c).wait()

    fwd = (
        [[pitch_ref[f, g] * -0.125 for g in range(F)] for f in range(F)],
        [[span_ref[f, g] * -0.125 for g in range(F)] for f in range(F)],
    )
    adj = (
        [[pitch_ref[g, f] * 0.125 for g in range(F)] for f in range(F)],
        [[span_ref[g, f] * 0.125 for g in range(F)] for f in range(F)],
    )
    keep = [1.0 - diff_ref[f] for f in range(F)]
    visc = [diff_ref[f] * 0.25 for f in range(F)]

    def no_halo(c):
        first_step(v0, v1, fwd, (M, E), False, c * per + 1, per)
        to_end((M,), True, c * per, per)
        stream_b(M, c).start()

    first_step(v0, v1, fwd, (M, E), False, per - 1, 2)
    no_halo(1)
    steps(0, blocks, pack_all, 8)
    for side in (0, 1):
        columns(side).start()

    @pl.loop(2, chunks - 1)
    def _(c):
        no_halo(c)

    for side in (0, 1):
        columns(side).wait()
    steps(0, blocks, unpack_all, 8)
    for side in (0, 1):
        edge_rows(0, side).start()
    first_step(v0, v1, fwd, (E, H), True, per - 1, blocks - 2 * per + 2)
    for side in (0, 1):
        edge_rows(0, side).wait()

    @pl.loop(0, 2)
    def _(i):
        first_step(v0, v1, fwd, (M, E, H), True, i * (blocks - per + 2) - 1, per)

    def both_ends(c):
        to_end((M, E), True, c * per, per)
        stream_b(M, c).start()
        stream_b(E, c).start()

    both_ends(0)
    both_ends(chunks - 1)

    def inward(j):
        lower = j % 2
        return 1 + j // 2 + lower * (chunks - 3 - j // 2 * 2), lower

    @pl.loop(0, chunks - 2)
    def _(j):
        c, _ = inward(j)
        to_end((E,), False, c * per, per)
        stream_b(E, c).start()

    def arrive(t, c):
        stream_a(t, c).wait_recv()

        for u in range(per):
            b = c * per + u
            part = pl.ds(row_at(b, 0), 8)
            for f in range(F):
                w0[t, f, pl.ds(row_at(b), 8), :] = end[t, f, part, :] - got_a[t, f, part, :]

    def out_rows(lo, count):
        def run(b, n):
            for u in range(n):
                part = pl.ds(row_at(b + u, 0), 8)
                for f in range(F):
                    one, two = rotate_out(*[w0[t, f, pl.ds(row_at(b + u), 8), :] for t in (M, E)])
                    mis_out[0, f, part, 0:L] = one
                    mis_out[0, f, part, L : 2 * L] = two

        steps(lo, count, run)

    def adjoint_rows(lo, count):
        def emit(b, total):
            part = pl.ds(row_at(b, 0), 8)
            for f in range(F):
                one, two = rotate_out(*[
                    total[t][f] - (got_b[t, f, part, :] - v0[t, f, pl.ds(row_at(b), 8), :]) for t in (M, E)
                ])
                grad_out[0, f, part, 0:L] = one
                grad_out[0, f, part, L : 2 * L] = two

        steps(lo, count, lambda b, n: stencil(w1, adj, b, n, (M, E), True, emit))

    send_pair(0)
    arrive(M, 0)
    arrive(M, chunks - 1)
    send_pair(1)
    take_pair(0)
    for side in (0, 1):
        edge_rows(1, side).start()
    send_pair(2)
    take_pair(1)
    for side in (0, 1):
        edge_rows(1, side).wait()
    send_pair(3)
    take_pair(2)

    def arrive_b(c):
        stream_b(M, c).wait_recv()
        stream_b(E, c).wait_recv()

    @pl.loop(0, 2)
    def _(i):
        first_step(w0, w1, adj, (M, E, H), True, i * (blocks - per + 2) - 1, per)
        out_rows(i * (blocks - per), per)
        arrive_b(i * (chunks - 1))
        adjoint_rows(i * (blocks - per + 2), per - 2)

    def inner_step(j):
        c, lower = inward(j)
        arrive(M, c)
        first_step(w0, w1, adj, (M, E, H), True, c * per - 1 + 2 * lower, per)
        out_rows(c * per, per)
        arrive_b(c)
        adjoint_rows(c * per - 2 + 4 * lower, per)

    pl.loop(0, 2)(inner_step)
    take_pair(3)
    pl.loop(2, chunks - 3)(inner_step)

    arrive(M, half)
    first_step(w0, w1, adj, (M, E, H), True, half * per - 1, per + 2)
    out_rows(half * per, per)

    def keep_adjoint(b, total):
        for f in range(F):
            for t in (M, E):
                w0[t, f, pl.ds(row_at(b), 8), :] = total[t][f]

    steps(half * per - 2, per + 4, lambda b, n: stencil(w1, adj, b, n, (M, E), True, keep_adjoint))
    arrive_b(half)

    def last_rows(b, n):
        for u in range(n):
            part = pl.ds(row_at(b + u, 0), 8)
            tall = pl.ds(row_at(b + u), 8)
            for f in range(F):
                one, two = rotate_out(*[
                    w0[t, f, tall, :] - (got_b[t, f, part, :] - v0[t, f, tall, :]) for t in (M, E)
                ])
                grad_out[0, f, part, 0:L] = one
                grad_out[0, f, part, L : 2 * L] = two

    steps(half * per - 2, per + 4, last_rows)

    for t in (M, E):
        @pl.loop(0, chunks)
        def _(c):
            stream_a(t, c).wait_send()
            stream_b(t, c).wait_send()


def store(mis, grad, mis_out, grad_out, sem):
    copies = [
        pltpu.make_async_copy(src.at[0, f], dst.at[0, f], sem.at[i, f])
        for f in range(F)
        for i, (src, dst) in enumerate(((mis, mis_out), (grad, grad_out)))
    ]
    for copy in copies:
        copy.start()
    for copy in copies:
        copy.wait()


def body(states, forcing, adv_pitch, adv_span, diffusion):
    states, forcing, adv_pitch, adv_span, diffusion = (
        pltpu.with_memory_space_constraint(x, pltpu.HBM) for x in (states, forcing, adv_pitch, adv_span, diffusion)
    )
    rows = states.shape[2]
    chunks = rows // CH
    tall = rows + 2 * PAD
    shape = jax.ShapeDtypeStruct(states.shape, jnp.float32)
    dma = pltpu.SemaphoreType.DMA
    tiles = pltpu.VMEM((3, F, tall, L), jnp.float32)
    pair = pltpu.VMEM((2, F, rows, L), jnp.float32)
    block = pltpu.VMEM((F, rows, 2 * L), jnp.float32)
    results = pl.pallas_call(
        kernel,
        out_shape=(shape, shape),
        in_specs=[pl.BlockSpec(memory_space=pltpu.HBM)] * 5,
        out_specs=[pl.BlockSpec(memory_space=pltpu.VMEM)] * 2,
        scratch_shapes=[
            pltpu.SMEM((F, F), jnp.float32), pltpu.SMEM((F, F), jnp.float32), pltpu.SMEM((F,), jnp.float32),
            block, block, pltpu.VMEM((2, 3, F, CH, L), jnp.float32), tiles, tiles, tiles, tiles, pair, pair, pair,
            pltpu.VMEM((rows, L), jnp.float32), pltpu.VMEM((chunks // 2, 2 * CH, L), jnp.float32),
            pltpu.VMEM((2, rows, L), jnp.float32), pltpu.VMEM((2, chunks // 2, 2 * CH, L), jnp.float32),
            dma((3,)), dma((chunks,)), dma((chunks,)),
            dma((2, chunks)), dma((2, chunks)), dma((2, chunks)), dma((2, chunks)),
            dma((2,)), dma((2,)), dma((chunks // 2, 2)), dma((chunks // 2, 2)), dma((2, 2)), dma((2, 2)),
        ],
        compiler_params=pltpu.CompilerParams(collective_id=0, has_side_effects=True, vmem_limit_bytes=40 << 20),
        name="orbit",
    )(states, forcing, adv_pitch, adv_span, diffusion)
    return pl.pallas_call(
        store,
        out_shape=(shape, shape),
        in_specs=[pl.BlockSpec(memory_space=pltpu.VMEM)] * 2,
        out_specs=[pl.BlockSpec(memory_space=pltpu.HBM)] * 2,
        scratch_shapes=[dma((2, F))],
        compiler_params=pltpu.CompilerParams(vmem_limit_bytes=4 << 20),
        name="store",
    )(*results)


def solution(mesh):
    spread = P("seg", None, "pitch", "span")
    return jax.shard_map(
        body,
        mesh=mesh,
        in_specs=(spread, spread, P(), P(), P()),
        out_specs=(spread, spread),
        check_vma=False,
    )
```

```python
import functools

import jax
import jax.numpy as jnp
from jax import lax
from jax.experimental import pallas as pl
from jax.experimental.pallas import tpu as pltpu
from jax.sharding import PartitionSpec as P

MESH = pl.DeviceIdType.MESH
F = 5
L = 128
PAD = 16
CH = 32
M, E, H = 0, 1, 2


def along(axis, by):
    count = lax.axis_size(axis)
    return {axis: lax.rem(lax.axis_index(axis) + (by + count), count)}


def rolled(x, by):
    return pltpu.roll(x, by % L, 1)


def kernel(
    states, forcing, pitch_hbm, span_hbm, diff_hbm, mis_out, grad_out,
    pitch_ref, span_ref, diff_ref, raw, force, across, v0, v1, w0, w1, end, got_a, got_b, packed, packed2, halo, halo2,
    load_c, load_s, load_f, a_send, a_recv, b_send, b_recv, col_send, col_recv, pair_send, pair_recv, row_send, row_recv,
    half_send, half_recv,
):
    rows = raw.shape[1]
    chunks = rows // CH
    assert chunks == 8
    blocks = rows // 8
    per = CH // 8
    half = chunks // 2
    outer_first = [c for i in range(half) for c in (i, chunks - 1 - i)]
    a_order = [(t, c) for part in (outer_first[:2], outer_first[2:]) for t in (E, M) for c in part if (t, c) != (M, half)]

    def load(src, dst, sem, c):
        part = pl.ds(c * CH, CH)
        return pltpu.make_async_copy(src.at[0, :, part], dst.at[:, part], sem.at[c])

    for c in range(chunks):
        load(states, raw, load_s, c).start()
    load(forcing, force, load_f, 1).start()
    coefs = [
        pltpu.make_async_copy(src, dst, load_c.at[i])
        for i, (src, dst) in enumerate(((pitch_hbm, pitch_ref), (span_hbm, span_ref), (diff_hbm, diff_ref)))
    ]
    for copy in coefs:
        copy.start()

    barrier = pltpu.get_barrier_semaphore()
    for axis in ("seg", "pitch", "span"):
        for by in (1, -1):
            pl.semaphore_signal(barrier, inc=1, device_id=along(axis, by), device_id_type=MESH)

    lane = lax.broadcasted_iota(jnp.int32, (8, L), 1)
    low = lane < 64
    span_at, span_of = lax.axis_index("span"), lax.axis_size("span")
    has_left = jnp.where(span_at > 0, 1, 0)
    has_right = jnp.where(span_at < span_of - 1, 1, 0)
    inside = jnp.where(low, has_left, has_right) > 0
    packed_left = (lane & 3) >= 2
    packed_inside = jnp.where(packed_left, has_left, has_right) > 0

    def rotate_in(first, second):
        one, two = rolled(first, 64), rolled(second, 64)
        return jnp.where(low, one, two), jnp.where(low, two, one)

    def rotate_out(mid, edge):
        one, two = rolled(mid, 64), rolled(edge, 64)
        return jnp.where(low, two, one), jnp.where(low, one, two)

    def steps(lo, count, run, size=4):
        if count // size:
            @pl.loop(0, count // size)
            def _(i):
                run(lo + i * size, size)
        if count % size:
            run(lo + count // size * size, count % size)

    def row_at(b, pad=PAD):
        return pl.multiple_of(b * 8 + pad, 8)

    def stencil(src, mats, b, n, outs, seam, emit):
        along_pitch, along_span = mats
        for u in range(n):
            part = slice(u * 8, u * 8 + 8)
            for g in range(F):
                right, left = {}, {}
                for t in (M, E, H) if seam else (M, E):
                    here = src[t, g, pl.ds(row_at(b + u), 8), :]
                    right[t] = rolled(here, -1)
                    left[t] = rolled(here, 1)
                for t in outs:
                    if t == M:
                        rt = jnp.where(lane == 127, right[E], right[M])
                        lf = jnp.where(lane == 0, left[E], left[M])
                    elif t == E:
                        rt = jnp.where(lane == 127, right[M], right[E])
                        lf = jnp.where(lane == 0, left[M], left[E])
                        if seam:
                            rt = jnp.where(lane == 63, right[H], rt)
                            lf = jnp.where(lane == 64, left[H], lf)
                    else:
                        rt = jnp.where(lane == 63, right[E], right[H])
                        lf = jnp.where(lane == 64, left[E], left[H])
                    across[0, t, g, part, :] = rt - lf
                    across[1, t, g, part, :] = rt + lf
        for u in range(n):
            e = row_at(b + u)
            part = slice(u * 8, u * 8 + 8)
            total = {t: [None] * F for t in outs}
            for g in range(F):
                for t in outs:
                    up = src[t, g, pl.ds(e + 1, 8), :]
                    dn = src[t, g, pl.ds(e - 1, 8), :]
                    dp, ds = up - dn, across[0, t, g, part, :]
                    around = (up + dn) + across[1, t, g, part, :]
                    for f in range(F):
                        term = along_pitch[f][g] * dp + along_span[f][g] * ds
                        if f == g:
                            term = term + (keep[g] * src[t, g, pl.ds(e, 8), :] + visc[g] * around)
                        total[t][f] = term if total[t][f] is None else total[t][f] + term
            emit(b + u, total)

    def first_step(src, dst, mats, outs, seam, lo, count):
        def emit(b, total):
            for t in outs:
                for f in range(F):
                    value = total[t][f]
                    if t == H:
                        value = jnp.where(inside, value, 0.0)
                    dst[t, f, pl.ds(row_at(b), 8), :] = value

        steps(lo, count, lambda b, n: stencil(src, mats, b, n, outs, seam, emit))

    def to_end(outs, fresh, lo, count):
        def emit(b, total):
            part = pl.ds(row_at(b, 0), 8)
            for f in range(F):
                for t in outs:
                    end[t, f, part, :] = total[t][f] + end[t, f, part, :]

        def run(b, n):
            if fresh:
                for u in range(n):
                    part = pl.ds(row_at(b + u, 0), 8)
                    for f in range(F):
                        both = rotate_in(force[f, part, 0:L], force[f, part, L : 2 * L])
                        end[M, f, part, :] = 0.25 * both[M]
                        end[E, f, part, :] = 0.25 * both[E]
            stencil(v1, fwd, b, n, outs, E in outs, emit)

        steps(lo, count, run)

    def stream_a(t, c):
        return pltpu.make_async_remote_copy(
            src_ref=v0.at[t, :, pl.ds(pl.multiple_of(c * CH + PAD, 8), CH)],
            dst_ref=got_a.at[t, :, pl.ds(pl.multiple_of(c * CH, 8), CH)],
            send_sem=a_send.at[t, c], recv_sem=a_recv.at[t, c],
            device_id=along("seg", -1), device_id_type=MESH,
        )

    def half_chunk(i):
        first = half * CH + i * CH // 2
        return pltpu.make_async_remote_copy(
            src_ref=v0.at[M, :, pl.ds(PAD + first, CH // 2)], dst_ref=got_a.at[M, :, pl.ds(first, CH // 2)],
            send_sem=half_send.at[i], recv_sem=half_recv.at[i],
            device_id=along("seg", -1), device_id_type=MESH,
        )

    def stream_b(t, c):
        part = pl.ds(pl.multiple_of(c * CH, 8), CH)
        return pltpu.make_async_remote_copy(
            src_ref=end.at[t, :, part], dst_ref=got_b.at[t, :, part],
            send_sem=b_send.at[t, c], recv_sem=b_recv.at[t, c],
            device_id=along("seg", 1), device_id_type=MESH,
        )

    def columns(side):
        return pltpu.make_async_remote_copy(
            src_ref=packed, dst_ref=halo.at[side],
            send_sem=col_send.at[side], recv_sem=col_recv.at[side],
            device_id=along("span", (1, -1)[side]), device_id_type=MESH,
        )

    def pair_columns(k, side):
        return pltpu.make_async_remote_copy(
            src_ref=packed2.at[k], dst_ref=halo2.at[side, k],
            send_sem=pair_send.at[k, side], recv_sem=pair_recv.at[k, side],
            device_id=along("span", (1, -1)[side]), device_id_type=MESH,
        )

    def edge_rows(phase, side):
        field = (v0, w0)[phase]
        if side == 0:
            src, dst = pl.ds(PAD + rows - 8, 8), pl.ds(PAD - 8, 8)
        else:
            src, dst = pl.ds(PAD, 8), pl.ds(PAD + rows, 8)
        return pltpu.make_async_remote_copy(
            src_ref=field.at[:, :, src], dst_ref=field.at[:, :, dst],
            send_sem=row_send.at[phase, side], recv_sem=row_recv.at[phase, side],
            device_id=along("pitch", (1, -1)[side]), device_id_type=MESH,
        )

    def pack_block(field, b):
        value = field[E, 2, pl.ds(row_at(b), 8), :]
        for f in (0, 1, 3, 4):
            at = 54 + 4 * f
            mine = (lane >= at) & (lane < at + 4)
            value = jnp.where(mine, rolled(field[E, f, pl.ds(row_at(b), 8), :], 4 * (f - 2)), value)
        return value

    def unpack_block(from_left, from_right, field, b):
        value = jnp.where(packed_left, from_left, from_right)
        value = jnp.where(packed_inside, value, 0.0)
        for f in range(F):
            field[H, f, pl.ds(row_at(b), 8), :] = rolled(value, -4 * (f - 2))

    def pack_all(b, n):
        for u in range(n):
            packed[pl.ds(row_at(b + u, 0), 8), :] = pack_block(v0, b + u)

    def unpack_all(b, n):
        for u in range(n):
            part = pl.ds(row_at(b + u, 0), 8)
            unpack_block(halo[0, part, :], halo[1, part, :], v0, b + u)

    def pair_blocks(k):
        return [(c * per + u, slice(i * CH + u * 8, i * CH + u * 8 + 8))
                for i, c in enumerate((k, chunks - 1 - k)) for u in range(per)]

    def send_pair(k):
        arrive(E, k)
        arrive(E, chunks - 1 - k)
        for b, part in pair_blocks(k):
            packed2[k, part, :] = pack_block(w0, b)
        for side in (0, 1):
            pair_columns(k, side).start()

    def take_pair(k):
        for side in (0, 1):
            pair_columns(k, side).wait()
        for b, part in pair_blocks(k):
            unpack_block(halo2[0, k, part, :], halo2[1, k, part, :], w0, b)

    @pl.loop(0, chunks)
    def _(c):
        load(states, raw, load_s, c).wait()
        for u in range(per):
            b = c * per + u
            part = pl.ds(row_at(b, 0), 8)
            for f in range(F):
                mid, edge = rotate_in(raw[f, part, 0:L], raw[f, part, L : 2 * L])
                v0[M, f, pl.ds(row_at(b), 8), :] = mid
                v0[E, f, pl.ds(row_at(b), 8), :] = edge

    for c in [0] + list(range(2, chunks)):
        load(forcing, force, load_f, c).start()
    for copy in coefs:
        copy.wait()

    fwd = (
        [[pitch_ref[f, g] * -0.125 for g in range(F)] for f in range(F)],
        [[span_ref[f, g] * -0.125 for g in range(F)] for f in range(F)],
    )
    adj = (
        [[pitch_ref[g, f] * 0.125 for g in range(F)] for f in range(F)],
        [[span_ref[g, f] * 0.125 for g in range(F)] for f in range(F)],
    )
    keep = [1.0 - diff_ref[f] for f in range(F)]
    visc = [diff_ref[f] * 0.25 for f in range(F)]

    def no_halo(c):
        first_step(v0, v1, fwd, (M, E), False, c * per + 1, per)
        to_end((M,), True, c * per, per)

    first_step(v0, v1, fwd, (M, E), False, per - 1, 2)
    load(forcing, force, load_f, 1).wait()
    no_halo(1)
    pl.semaphore_wait(barrier, 6)
    stream_b(M, 1).start()
    for t, c in a_order:
        stream_a(t, c).start()
    for i in (1, 0):
        half_chunk(i).start()
    for c in [0] + list(range(2, chunks)):
        load(forcing, force, load_f, c).wait()
    steps(0, blocks, pack_all, 8)
    for side in (0, 1):
        columns(side).start()

    @pl.loop(2, chunks - 1)
    def _(c):
        no_halo(c)
        stream_b(M, c).start()

    for side in (0, 1):
        columns(side).wait()
    steps(0, blocks, unpack_all, 8)
    for side in (0, 1):
        edge_rows(0, side).start()
    first_step(v0, v1, fwd, (E, H), True, per - 1, blocks - 2 * per + 2)
    for side in (0, 1):
        edge_rows(0, side).wait()

    @pl.loop(0, 2)
    def _(i):
        first_step(v0, v1, fwd, (M, E, H), True, i * (blocks - per + 2) - 1, per)

    def both_ends(c):
        to_end((M, E), True, c * per, per)
        stream_b(M, c).start()
        stream_b(E, c).start()

    both_ends(0)
    both_ends(chunks - 1)

    def inward(j):
        lower = j % 2
        return 1 + j // 2 + lower * (chunks - 3 - j // 2 * 2), lower

    @pl.loop(0, chunks - 2)
    def _(j):
        c, _ = inward(j)
        to_end((E,), False, c * per, per)
        stream_b(E, c).start()

    def take_mismatch(t, b, n):
        for u in range(n):
            part = pl.ds(row_at(b + u, 0), 8)
            for f in range(F):
                w0[t, f, pl.ds(row_at(b + u), 8), :] = end[t, f, part, :] - got_a[t, f, part, :]

    def arrive(t, c):
        stream_a(t, c).wait_recv()
        take_mismatch(t, c * per, per)

    def out_rows(lo, count):
        def run(b, n):
            for u in range(n):
                part = pl.ds(row_at(b + u, 0), 8)
                for f in range(F):
                    one, two = rotate_out(*[w0[t, f, pl.ds(row_at(b + u), 8), :] for t in (M, E)])
                    mis_out[0, f, part, 0:L] = one
                    mis_out[0, f, part, L : 2 * L] = two

        steps(lo, count, run)

    def adjoint_rows(lo, count):
        def emit(b, total):
            part = pl.ds(row_at(b, 0), 8)
            for f in range(F):
                one, two = rotate_out(*[
                    total[t][f] - (got_b[t, f, part, :] - v0[t, f, pl.ds(row_at(b), 8), :]) for t in (M, E)
                ])
                grad_out[0, f, part, 0:L] = one
                grad_out[0, f, part, L : 2 * L] = two

        steps(lo, count, lambda b, n: stencil(w1, adj, b, n, (M, E), True, emit))

    send_pair(0)
    arrive(M, 0)
    arrive(M, chunks - 1)
    send_pair(1)
    take_pair(0)
    for side in (0, 1):
        edge_rows(1, side).start()
    send_pair(2)
    take_pair(1)
    for side in (0, 1):
        edge_rows(1, side).wait()
    send_pair(3)
    take_pair(2)

    def arrive_b(c):
        stream_b(M, c).wait_recv()
        stream_b(E, c).wait_recv()

    @pl.loop(0, 2)
    def _(i):
        first_step(w0, w1, adj, (M, E, H), True, i * (blocks - per + 2) - 1, per)
        out_rows(i * (blocks - per), per)
        arrive_b(i * (chunks - 1))
        adjoint_rows(i * (blocks - per + 2), per - 2)

    def inner_step(j):
        c, lower = inward(j)
        arrive(M, c)
        first_step(w0, w1, adj, (M, E, H), True, c * per - 1 + 2 * lower, per)
        out_rows(c * per, per)
        arrive_b(c)
        adjoint_rows(c * per - 2 + 4 * lower, per)

    pl.loop(0, 2)(inner_step)
    take_pair(3)
    pl.loop(2, chunks - 3)(inner_step)

    at = half * per
    first_step(w0, w1, adj, (H,), True, at - 1, per + 2)
    for c in range(chunks):
        stream_a(E, c).wait_send()
        stream_b(M, c).wait_send()
    half_chunk(1).wait_recv()
    take_mismatch(M, at + per // 2, per // 2)
    first_step(w0, w1, adj, (M, E), True, at + per - 1, 2)
    adjoint_rows(at + per, 2)
    half_chunk(0).wait_recv()
    take_mismatch(M, at, per // 2)
    first_step(w0, w1, adj, (M, E), True, at - 1, per)
    out_rows(at, per)

    def keep_adjoint(b, total):
        for f in range(F):
            for t in (M, E):
                w0[t, f, pl.ds(row_at(b), 8), :] = total[t][f]

    steps(at - 2, per + 2, lambda b, n: stencil(w1, adj, b, n, (M, E), True, keep_adjoint))
    arrive_b(half)

    def last_rows(b, n):
        for u in range(n):
            part = pl.ds(row_at(b + u, 0), 8)
            tall = pl.ds(row_at(b + u), 8)
            for f in range(F):
                one, two = rotate_out(*[
                    w0[t, f, tall, :] - (got_b[t, f, part, :] - v0[t, f, tall, :]) for t in (M, E)
                ])
                grad_out[0, f, part, 0:L] = one
                grad_out[0, f, part, L : 2 * L] = two

    steps(at - 2, per + 2, last_rows)

    for i in (0, 1):
        half_chunk(i).wait_send()

    @pl.loop(0, chunks - 1)
    def _(i):
        stream_a(M, jnp.where(i < half, i, i + 1)).wait_send()

    @pl.loop(0, chunks)
    def _(c):
        stream_b(E, c).wait_send()


def store(mis, grad, mis_out, grad_out, sem):
    copies = [
        pltpu.make_async_copy(src.at[0, f], dst.at[0, f], sem.at[i, f])
        for f in range(F)
        for i, (src, dst) in enumerate(((mis, mis_out), (grad, grad_out)))
    ]
    for copy in copies:
        copy.start()
    for copy in copies:
        copy.wait()


def body(states, forcing, adv_pitch, adv_span, diffusion):
    states, forcing, adv_pitch, adv_span, diffusion = (
        pltpu.with_memory_space_constraint(x, pltpu.HBM) for x in (states, forcing, adv_pitch, adv_span, diffusion)
    )
    rows = states.shape[2]
    chunks = rows // CH
    tall = rows + 2 * PAD
    shape = jax.ShapeDtypeStruct(states.shape, jnp.float32)
    dma = pltpu.SemaphoreType.DMA
    tiles = pltpu.VMEM((3, F, tall, L), jnp.float32)
    pair = pltpu.VMEM((2, F, rows, L), jnp.float32)
    block = pltpu.VMEM((F, rows, 2 * L), jnp.float32)
    results = pl.pallas_call(
        kernel,
        out_shape=(shape, shape),
        in_specs=[pl.BlockSpec(memory_space=pltpu.HBM)] * 5,
        out_specs=[pl.BlockSpec(memory_space=pltpu.VMEM)] * 2,
        scratch_shapes=[
            pltpu.SMEM((F, F), jnp.float32), pltpu.SMEM((F, F), jnp.float32), pltpu.SMEM((F,), jnp.float32),
            block, block, pltpu.VMEM((2, 3, F, CH, L), jnp.float32), tiles, tiles, tiles, tiles, pair, pair, pair,
            pltpu.VMEM((rows, L), jnp.float32), pltpu.VMEM((chunks // 2, 2 * CH, L), jnp.float32),
            pltpu.VMEM((2, rows, L), jnp.float32), pltpu.VMEM((2, chunks // 2, 2 * CH, L), jnp.float32),
            dma((3,)), dma((chunks,)), dma((chunks,)),
            dma((2, chunks)), dma((2, chunks)), dma((2, chunks)), dma((2, chunks)),
            dma((2,)), dma((2,)), dma((chunks // 2, 2)), dma((chunks // 2, 2)), dma((2, 2)), dma((2, 2)),
            dma((2,)), dma((2,)),
        ],
        compiler_params=pltpu.CompilerParams(collective_id=0, has_side_effects=True, vmem_limit_bytes=40 << 20),
        name="orbit",
    )(states, forcing, adv_pitch, adv_span, diffusion)
    return pl.pallas_call(
        store,
        out_shape=(shape, shape),
        in_specs=[pl.BlockSpec(memory_space=pltpu.VMEM)] * 2,
        out_specs=[pl.BlockSpec(memory_space=pltpu.HBM)] * 2,
        scratch_shapes=[dma((2, F))],
        compiler_params=pltpu.CompilerParams(vmem_limit_bytes=4 << 20),
        name="store",
    )(*results)


def solution(mesh):
    spread = P("seg", None, "pitch", "span")
    return jax.shard_map(
        body,
        mesh=mesh,
        in_specs=(spread, spread, P(), P(), P()),
        out_specs=(spread, spread),
        check_vma=False,
    )
```

```python
import functools

import jax
import jax.numpy as jnp
from jax import lax
from jax.experimental import pallas as pl
from jax.experimental.pallas import tpu as pltpu
from jax.sharding import PartitionSpec as P

MESH = pl.DeviceIdType.MESH
F = 5
L = 128
PAD = 16
CH = 32
M, E, H = 0, 1, 2


def along(axis, by):
    count = lax.axis_size(axis)
    return {axis: lax.rem(lax.axis_index(axis) + (by + count), count)}


def rolled(x, by):
    return pltpu.roll(x, by % L, 1)


def kernel(
    states, forcing, pitch_hbm, span_hbm, diff_hbm, mis_out, grad_out,
    pitch_ref, span_ref, diff_ref, raw, force, across, v0, v1, w0, w1, end, got_a, got_b, packed, packed2, halo, halo2,
    load_c, load_s, load_f, a_send, a_recv, b_send, b_recv, col_send, col_recv, pair_send, pair_recv, row_send, row_recv,
    half_send, half_recv,
):
    rows = raw.shape[1]
    chunks = rows // CH
    assert chunks == 8
    blocks = rows // 8
    per = CH // 8
    half = chunks // 2
    outer_first = [c for i in range(half) for c in (i, chunks - 1 - i)]
    a_order = [(t, c) for part in (outer_first[:2], outer_first[2:]) for t in (E, M) for c in part if (t, c) != (M, half)]

    def load(src, dst, sem, c):
        part = pl.ds(c * CH, CH)
        return pltpu.make_async_copy(src.at[0, :, part], dst.at[:, part], sem.at[c])

    barrier = pltpu.get_barrier_semaphore()
    for axis in ("seg", "pitch", "span"):
        for by in (1, -1):
            pl.semaphore_signal(barrier, inc=1, device_id=along(axis, by), device_id_type=MESH)

    for c in range(chunks):
        load(states, raw, load_s, c).start()
    load(forcing, force, load_f, 1).start()
    coefs = [
        pltpu.make_async_copy(src, dst, load_c.at[i])
        for i, (src, dst) in enumerate(((pitch_hbm, pitch_ref), (span_hbm, span_ref), (diff_hbm, diff_ref)))
    ]
    for copy in coefs:
        copy.start()

    lane = lax.broadcasted_iota(jnp.int32, (8, L), 1)
    low = lane < 64
    span_at, span_of = lax.axis_index("span"), lax.axis_size("span")
    has_left = jnp.where(span_at > 0, 1, 0)
    has_right = jnp.where(span_at < span_of - 1, 1, 0)
    inside = jnp.where(low, has_left, has_right) > 0
    packed_left = (lane & 3) >= 2
    packed_inside = jnp.where(packed_left, has_left, has_right) > 0

    def rotate_in(first, second):
        one, two = rolled(first, 64), rolled(second, 64)
        return jnp.where(low, one, two), jnp.where(low, two, one)

    def rotate_out(mid, edge):
        one, two = rolled(mid, 64), rolled(edge, 64)
        return jnp.where(low, two, one), jnp.where(low, one, two)

    def steps(lo, count, run, size=4):
        if count // size:
            @pl.loop(0, count // size)
            def _(i):
                run(lo + i * size, size)
        if count % size:
            run(lo + count // size * size, count % size)

    def row_at(b, pad=PAD):
        return pl.multiple_of(b * 8 + pad, 8)

    def stencil(src, mats, b, n, outs, seam, emit):
        along_pitch, along_span = mats
        for u in range(n):
            part = slice(u * 8, u * 8 + 8)
            for g in range(F):
                right, left = {}, {}
                for t in (M, E, H) if seam else (M, E):
                    here = src[t, g, pl.ds(row_at(b + u), 8), :]
                    right[t] = rolled(here, -1)
                    left[t] = rolled(here, 1)
                for t in outs:
                    if t == M:
                        rt = jnp.where(lane == 127, right[E], right[M])
                        lf = jnp.where(lane == 0, left[E], left[M])
                    elif t == E:
                        rt = jnp.where(lane == 127, right[M], right[E])
                        lf = jnp.where(lane == 0, left[M], left[E])
                        if seam:
                            rt = jnp.where(lane == 63, right[H], rt)
                            lf = jnp.where(lane == 64, left[H], lf)
                    else:
                        rt = jnp.where(lane == 63, right[E], right[H])
                        lf = jnp.where(lane == 64, left[E], left[H])
                    across[0, t, g, part, :] = rt - lf
                    across[1, t, g, part, :] = rt + lf
        for u in range(n):
            e = row_at(b + u)
            part = slice(u * 8, u * 8 + 8)
            total = {t: [None] * F for t in outs}
            for g in range(F):
                for t in outs:
                    up = src[t, g, pl.ds(e + 1, 8), :]
                    dn = src[t, g, pl.ds(e - 1, 8), :]
                    dp, ds = up - dn, across[0, t, g, part, :]
                    around = (up + dn) + across[1, t, g, part, :]
                    for f in range(F):
                        term = along_pitch[f][g] * dp + along_span[f][g] * ds
                        if f == g:
                            term = term + (keep[g] * src[t, g, pl.ds(e, 8), :] + visc[g] * around)
                        total[t][f] = term if total[t][f] is None else total[t][f] + term
            emit(b + u, total)

    def first_step(src, dst, mats, outs, seam, lo, count):
        def emit(b, total):
            for t in outs:
                for f in range(F):
                    value = total[t][f]
                    if t == H:
                        value = jnp.where(inside, value, 0.0)
                    dst[t, f, pl.ds(row_at(b), 8), :] = value

        steps(lo, count, lambda b, n: stencil(src, mats, b, n, outs, seam, emit))

    def to_end(outs, fresh, lo, count):
        def emit(b, total):
            part = pl.ds(row_at(b, 0), 8)
            for f in range(F):
                for t in outs:
                    end[t, f, part, :] = total[t][f] + end[t, f, part, :]

        def run(b, n):
            if fresh:
                for u in range(n):
                    part = pl.ds(row_at(b + u, 0), 8)
                    for f in range(F):
                        both = rotate_in(force[f, part, 0:L], force[f, part, L : 2 * L])
                        end[M, f, part, :] = 0.25 * both[M]
                        end[E, f, part, :] = 0.25 * both[E]
            stencil(v1, fwd, b, n, outs, E in outs, emit)

        steps(lo, count, run)

    def stream_a(t, c):
        return pltpu.make_async_remote_copy(
            src_ref=v0.at[t, :, pl.ds(pl.multiple_of(c * CH + PAD, 8), CH)],
            dst_ref=got_a.at[t, :, pl.ds(pl.multiple_of(c * CH, 8), CH)],
            send_sem=a_send.at[t, c], recv_sem=a_recv.at[t, c],
            device_id=along("seg", -1), device_id_type=MESH,
        )

    def half_chunk(i):
        first = half * CH + i * CH // 2
        return pltpu.make_async_remote_copy(
            src_ref=v0.at[M, :, pl.ds(PAD + first, CH // 2)], dst_ref=got_a.at[M, :, pl.ds(first, CH // 2)],
            send_sem=half_send.at[i], recv_sem=half_recv.at[i],
            device_id=along("seg", -1), device_id_type=MESH,
        )

    def stream_b(t, c):
        part = pl.ds(pl.multiple_of(c * CH, 8), CH)
        return pltpu.make_async_remote_copy(
            src_ref=end.at[t, :, part], dst_ref=got_b.at[t, :, part],
            send_sem=b_send.at[t, c], recv_sem=b_recv.at[t, c],
            device_id=along("seg", 1), device_id_type=MESH,
        )

    def columns(side):
        return pltpu.make_async_remote_copy(
            src_ref=packed, dst_ref=halo.at[side],
            send_sem=col_send.at[side], recv_sem=col_recv.at[side],
            device_id=along("span", (1, -1)[side]), device_id_type=MESH,
        )

    def pair_columns(k, side):
        return pltpu.make_async_remote_copy(
            src_ref=packed2.at[k], dst_ref=halo2.at[side, k],
            send_sem=pair_send.at[k, side], recv_sem=pair_recv.at[k, side],
            device_id=along("span", (1, -1)[side]), device_id_type=MESH,
        )

    def edge_rows(phase, side):
        field = (v0, w0)[phase]
        if side == 0:
            src, dst = pl.ds(PAD + rows - 8, 8), pl.ds(PAD - 8, 8)
        else:
            src, dst = pl.ds(PAD, 8), pl.ds(PAD + rows, 8)
        return pltpu.make_async_remote_copy(
            src_ref=field.at[:, :, src], dst_ref=field.at[:, :, dst],
            send_sem=row_send.at[phase, side], recv_sem=row_recv.at[phase, side],
            device_id=along("pitch", (1, -1)[side]), device_id_type=MESH,
        )

    def pack_block(field, b):
        value = field[E, 2, pl.ds(row_at(b), 8), :]
        for f in (0, 1, 3, 4):
            at = 54 + 4 * f
            mine = (lane >= at) & (lane < at + 4)
            value = jnp.where(mine, rolled(field[E, f, pl.ds(row_at(b), 8), :], 4 * (f - 2)), value)
        return value

    def unpack_block(from_left, from_right, field, b):
        value = jnp.where(packed_left, from_left, from_right)
        value = jnp.where(packed_inside, value, 0.0)
        for f in range(F):
            field[H, f, pl.ds(row_at(b), 8), :] = rolled(value, -4 * (f - 2))

    def pack_all(b, n):
        for u in range(n):
            packed[pl.ds(row_at(b + u, 0), 8), :] = pack_block(v0, b + u)

    def unpack_all(b, n):
        for u in range(n):
            part = pl.ds(row_at(b + u, 0), 8)
            unpack_block(halo[0, part, :], halo[1, part, :], v0, b + u)

    def pair_blocks(k):
        return [(c * per + u, slice(i * CH + u * 8, i * CH + u * 8 + 8))
                for i, c in enumerate((k, chunks - 1 - k)) for u in range(per)]

    def send_pair(k):
        arrive(E, k)
        arrive(E, chunks - 1 - k)
        for b, part in pair_blocks(k):
            packed2[k, part, :] = pack_block(w0, b)
        for side in (0, 1):
            pair_columns(k, side).start()

    def take_pair(k):
        for side in (0, 1):
            pair_columns(k, side).wait()
        for b, part in pair_blocks(k):
            unpack_block(halo2[0, k, part, :], halo2[1, k, part, :], w0, b)

    @pl.loop(0, chunks)
    def _(c):
        load(states, raw, load_s, c).wait()
        for u in range(per):
            b = c * per + u
            part = pl.ds(row_at(b, 0), 8)
            for f in range(F):
                mid, edge = rotate_in(raw[f, part, 0:L], raw[f, part, L : 2 * L])
                v0[M, f, pl.ds(row_at(b), 8), :] = mid
                v0[E, f, pl.ds(row_at(b), 8), :] = edge

    for c in [0] + list(range(2, chunks)):
        load(forcing, force, load_f, c).start()
    for copy in coefs:
        copy.wait()

    fwd = (
        [[pitch_ref[f, g] * -0.125 for g in range(F)] for f in range(F)],
        [[span_ref[f, g] * -0.125 for g in range(F)] for f in range(F)],
    )
    adj = (
        [[pitch_ref[g, f] * 0.125 for g in range(F)] for f in range(F)],
        [[span_ref[g, f] * 0.125 for g in range(F)] for f in range(F)],
    )
    keep = [1.0 - diff_ref[f] for f in range(F)]
    visc = [diff_ref[f] * 0.25 for f in range(F)]

    def no_halo(c):
        first_step(v0, v1, fwd, (M, E), False, c * per + 1, per)
        to_end((M,), True, c * per, per)

    first_step(v0, v1, fwd, (M, E), False, per - 1, 2)
    load(forcing, force, load_f, 1).wait()
    no_halo(1)
    pl.semaphore_wait(barrier, 6)
    stream_b(M, 1).start()
    for t, c in a_order:
        stream_a(t, c).start()
    for i in (1, 0):
        half_chunk(i).start()
    for c in [0] + list(range(2, chunks)):
        load(forcing, force, load_f, c).wait()
    steps(0, blocks, pack_all, 8)
    for side in (0, 1):
        columns(side).start()

    @pl.loop(2, chunks - 1)
    def _(c):
        no_halo(c)
        stream_b(M, c).start()

    for side in (0, 1):
        columns(side).wait()
    steps(0, blocks, unpack_all, 8)
    for side in (0, 1):
        edge_rows(0, side).start()
    first_step(v0, v1, fwd, (E, H), True, per - 1, blocks - 2 * per + 2)
    for side in (0, 1):
        edge_rows(0, side).wait()

    @pl.loop(0, 2)
    def _(i):
        first_step(v0, v1, fwd, (M, E, H), True, i * (blocks - per + 2) - 1, per)

    def both_ends(c):
        to_end((M, E), True, c * per, per)
        stream_b(M, c).start()
        stream_b(E, c).start()

    both_ends(0)
    both_ends(chunks - 1)

    def inward(j):
        lower = j % 2
        return 1 + j // 2 + lower * (chunks - 3 - j // 2 * 2), lower

    @pl.loop(0, chunks - 2)
    def _(j):
        c, _ = inward(j)
        to_end((E,), False, c * per, per)
        stream_b(E, c).start()

    def take_mismatch(t, b, n):
        for u in range(n):
            part = pl.ds(row_at(b + u, 0), 8)
            for f in range(F):
                w0[t, f, pl.ds(row_at(b + u), 8), :] = end[t, f, part, :] - got_a[t, f, part, :]

    def arrive(t, c):
        stream_a(t, c).wait_recv()
        take_mismatch(t, c * per, per)

    def out_rows(lo, count):
        def run(b, n):
            for u in range(n):
                part = pl.ds(row_at(b + u, 0), 8)
                for f in range(F):
                    one, two = rotate_out(*[w0[t, f, pl.ds(row_at(b + u), 8), :] for t in (M, E)])
                    mis_out[0, f, part, 0:L] = one
                    mis_out[0, f, part, L : 2 * L] = two

        steps(lo, count, run)

    def adjoint_rows(lo, count):
        def emit(b, total):
            part = pl.ds(row_at(b, 0), 8)
            for f in range(F):
                one, two = rotate_out(*[
                    total[t][f] - (got_b[t, f, part, :] - v0[t, f, pl.ds(row_at(b), 8), :]) for t in (M, E)
                ])
                grad_out[0, f, part, 0:L] = one
                grad_out[0, f, part, L : 2 * L] = two

        steps(lo, count, lambda b, n: stencil(w1, adj, b, n, (M, E), True, emit))

    send_pair(0)
    arrive(M, 0)
    arrive(M, chunks - 1)
    send_pair(1)
    take_pair(0)
    for side in (0, 1):
        edge_rows(1, side).start()
    send_pair(2)
    take_pair(1)
    for side in (0, 1):
        edge_rows(1, side).wait()
    send_pair(3)
    take_pair(2)

    def arrive_b(c):
        stream_b(M, c).wait_recv()
        stream_b(E, c).wait_recv()

    @pl.loop(0, 2)
    def _(i):
        first_step(w0, w1, adj, (M, E, H), True, i * (blocks - per + 2) - 1, per)
        out_rows(i * (blocks - per), per)
        arrive_b(i * (chunks - 1))
        adjoint_rows(i * (blocks - per + 2), per - 2)

    def inner_step(j):
        c, lower = inward(j)
        arrive(M, c)
        first_step(w0, w1, adj, (M, E, H), True, c * per - 1 + 2 * lower, per)
        out_rows(c * per, per)
        arrive_b(c)
        adjoint_rows(c * per - 2 + 4 * lower, per)

    pl.loop(0, 2)(inner_step)
    take_pair(3)
    pl.loop(2, chunks - 3)(inner_step)

    at = half * per
    first_step(w0, w1, adj, (H,), True, at - 1, per + 2)
    for c in range(chunks):
        stream_a(E, c).wait_send()
        stream_b(M, c).wait_send()
    half_chunk(1).wait_recv()
    take_mismatch(M, at + per // 2, per // 2)
    first_step(w0, w1, adj, (M, E), True, at + per - 1, 2)
    adjoint_rows(at + per, 2)
    half_chunk(0).wait_recv()
    take_mismatch(M, at, per // 2)
    first_step(w0, w1, adj, (M, E), True, at - 1, per)
    out_rows(at, per)

    def keep_adjoint(b, total):
        for f in range(F):
            for t in (M, E):
                w0[t, f, pl.ds(row_at(b), 8), :] = total[t][f]

    steps(at - 2, per + 2, lambda b, n: stencil(w1, adj, b, n, (M, E), True, keep_adjoint))
    arrive_b(half)

    def last_rows(b, n):
        for u in range(n):
            part = pl.ds(row_at(b + u, 0), 8)
            tall = pl.ds(row_at(b + u), 8)
            for f in range(F):
                one, two = rotate_out(*[
                    w0[t, f, tall, :] - (got_b[t, f, part, :] - v0[t, f, tall, :]) for t in (M, E)
                ])
                grad_out[0, f, part, 0:L] = one
                grad_out[0, f, part, L : 2 * L] = two

    steps(at - 2, per + 2, last_rows)

    for i in (0, 1):
        half_chunk(i).wait_send()

    @pl.loop(0, chunks - 1)
    def _(i):
        stream_a(M, jnp.where(i < half, i, i + 1)).wait_send()

    @pl.loop(0, chunks)
    def _(c):
        stream_b(E, c).wait_send()


def store(mis, grad, mis_out, grad_out, sem):
    copies = [
        pltpu.make_async_copy(src.at[0, f], dst.at[0, f], sem.at[i, f])
        for f in range(F)
        for i, (src, dst) in enumerate(((mis, mis_out), (grad, grad_out)))
    ]
    for copy in copies:
        copy.start()
    for copy in copies:
        copy.wait()


def body(states, forcing, adv_pitch, adv_span, diffusion):
    states, forcing, adv_pitch, adv_span, diffusion = (
        pltpu.with_memory_space_constraint(x, pltpu.HBM) for x in (states, forcing, adv_pitch, adv_span, diffusion)
    )
    rows = states.shape[2]
    chunks = rows // CH
    tall = rows + 2 * PAD
    shape = jax.ShapeDtypeStruct(states.shape, jnp.float32)
    dma = pltpu.SemaphoreType.DMA
    tiles = pltpu.VMEM((3, F, tall, L), jnp.float32)
    pair = pltpu.VMEM((2, F, rows, L), jnp.float32)
    block = pltpu.VMEM((F, rows, 2 * L), jnp.float32)
    results = pl.pallas_call(
        kernel,
        out_shape=(shape, shape),
        in_specs=[pl.BlockSpec(memory_space=pltpu.HBM)] * 5,
        out_specs=[pl.BlockSpec(memory_space=pltpu.VMEM)] * 2,
        scratch_shapes=[
            pltpu.SMEM((F, F), jnp.float32), pltpu.SMEM((F, F), jnp.float32), pltpu.SMEM((F,), jnp.float32),
            block, block, pltpu.VMEM((2, 3, F, CH, L), jnp.float32), tiles, tiles, tiles, tiles, pair, pair, pair,
            pltpu.VMEM((rows, L), jnp.float32), pltpu.VMEM((chunks // 2, 2 * CH, L), jnp.float32),
            pltpu.VMEM((2, rows, L), jnp.float32), pltpu.VMEM((2, chunks // 2, 2 * CH, L), jnp.float32),
            dma((3,)), dma((chunks,)), dma((chunks,)),
            dma((2, chunks)), dma((2, chunks)), dma((2, chunks)), dma((2, chunks)),
            dma((2,)), dma((2,)), dma((chunks // 2, 2)), dma((chunks // 2, 2)), dma((2, 2)), dma((2, 2)),
            dma((2,)), dma((2,)),
        ],
        compiler_params=pltpu.CompilerParams(collective_id=0, has_side_effects=True, vmem_limit_bytes=40 << 20),
        name="orbit",
    )(states, forcing, adv_pitch, adv_span, diffusion)
    return pl.pallas_call(
        store,
        out_shape=(shape, shape),
        in_specs=[pl.BlockSpec(memory_space=pltpu.VMEM)] * 2,
        out_specs=[pl.BlockSpec(memory_space=pltpu.HBM)] * 2,
        scratch_shapes=[dma((2, F))],
        compiler_params=pltpu.CompilerParams(vmem_limit_bytes=4 << 20),
        name="store",
    )(*results)


def solution(mesh):
    spread = P("seg", None, "pitch", "span")
    return jax.shard_map(
        body,
        mesh=mesh,
        in_specs=(spread, spread, P(), P(), P()),
        out_specs=(spread, spread),
        check_vma=False,
    )
```
